32 devices in a mesh: param: 16 (over z, y, core), tm: 2 (over x).
Axes of the slice: x: 2, y: 2, z: 4, core: 2. Of those that a mesh axis runs over, the one named last changes fastest.
Arguments:
- params: bfloat16 [32, 32, 8192], P(None, 'tm', 'param'), may hold values from -6 to 6
- kernel: bfloat16 [8, 8192, 600], P(None, 'param'), may hold values from -0.0234375 to 0.0234375
- lag_offsets: int32 [8], replicated, may hold values from 0 to 11, as said below
- observed: bfloat16 [32, 32, 600], P(None, 'tm'), may hold values from -6 to 6
- diag_inverse: float32 [600, 600], replicated, may hold values from -2 to 2, as said below
- coupling: float32 [3, 600, 600], replicated, may hold values from -26 to 26
Outputs:
- whitened: float32 [32, 32, 600], P(None, 'tm')
The draws below stay inside these ranges and needn't reach their ends.
Inputs may be any that keep to these rules, and one draw needn't show every extreme that they name: `lag_offsets`: the offsets are distinct and one of them is always 12 - 1. `diag_inverse`: lower triangular with a positive diagonal.
All inputs are finite; a program needn't handle non-finite values.
Results may differ from the reference program's by a relative error of at most 0.0003.
Values may be sent and summed in bfloat16 or wider, within the bound.
A program may use at most 64 MiB of HBM per device.

```python
import math
import jax
import jax.numpy as jnp
from jax import lax

SENSORS = 600
LAGS = 8
REACH = 12
BAND = 4
SAMPLES = 32
PCOLS = 8192
STEPS = 32


def draw_lag_offsets(key, part):
    chosen = jax.random.permutation(key, REACH - 1)[:LAGS - 1]
    return jnp.concatenate([chosen, jnp.array([REACH - 1])]).astype(jnp.int32)


def noise_parts(key):
    keys = jax.random.split(jax.random.fold_in(key, 7), 4)
    count = SENSORS
    scales = jax.random.uniform(keys[0], (count,), jnp.float32, 0.05, 0.1)
    lower = jax.random.normal(keys[1], (count, count), jnp.float32) * (0.4 * 0.075 / count ** 0.5)
    rate_log = jax.random.uniform(keys[2], (count,), jnp.float32, math.log(0.5 / STEPS), math.log(1.0 / 15.0))
    retention = jnp.exp(-jnp.exp(rate_log))
    inverse_block = jnp.tril(lower, -1) + jnp.diag(scales)
    factor = jnp.linalg.solve(inverse_block, jnp.eye(count, dtype=jnp.float32))
    mixing = jax.random.normal(keys[3], (BAND - 1, count, count), jnp.float32) * (0.0025 / count ** 0.5)
    leading = mixing[0] - jnp.diag(retention)
    stacked = jnp.concatenate([leading[None], mixing[1:]], axis=0)
    coupled = jnp.einsum('mn,jnk->jmk', factor, stacked, precision=lax.Precision.HIGHEST)
    return (inverse_block.astype(jnp.float32), coupled.astype(jnp.float32))


def draw_diag_inverse(key, part):
    inverse_block, coupled = noise_parts(key)
    return inverse_block


def draw_coupling(key, part):
    inverse_block, coupled = noise_parts(key)
    return coupled


def shard_levels(rng, dims, shards, low, largest):
    gain, own = 1.0, jax.random.fold_in(rng, 6)
    for position, shards_of in shards:
        draws = jnp.exp(jax.random.uniform(jax.random.fold_in(own, position), (shards_of,), jnp.float32, low / len(shards), largest / len(shards)))
        gain = gain * jnp.repeat(draws, dims[position] // shards_of).reshape([-1 if axis == position else 1 for axis in range(len(dims))])
    return gain


def gaussian(own_key, extent, scale, reach, pieces=(), held_as=jnp.bfloat16):
    values = scale * jax.random.normal(own_key, extent, jnp.float32)
    if pieces:
        values = values * shard_levels(own_key, extent, pieces, -0.22, 0.18)
    return jnp.clip(values, -reach, reach).astype(held_as)


def setup_inputs(seed: int = 0) -> dict:
    splits = jax.random.split(jax.random.key(seed), 7)
    return {
        "params": gaussian(splits[0], (SAMPLES, STEPS, PCOLS), 1.0, 6.0, ((1, 2), (2, 16))),
        "kernel": gaussian(splits[1], (LAGS, PCOLS, SENSORS), (LAGS * PCOLS) ** -0.5, 0.0234375, ((1, 16),)),
        "lag_offsets": draw_lag_offsets(jax.random.fold_in(splits[6], 71), 0),
        "observed": gaussian(splits[3], (SAMPLES, STEPS, SENSORS), 1.0, 6.0, ((1, 2),)),
        "diag_inverse": draw_diag_inverse(jax.random.fold_in(splits[6], 71), 0),
        "coupling": draw_coupling(jax.random.fold_in(splits[6], 71), 0),
    }


def reference(params, kernel, lag_offsets, observed, diag_inverse, coupling):
    padded = jnp.pad(params, ((0, 0), (REACH - 1, 0), (0, 0)))
    predicted = jnp.zeros((SAMPLES, STEPS, SENSORS), jnp.float32)
    for lag_index in range(LAGS):
        start = (REACH - 1 - lag_offsets[lag_index]).astype(jnp.int32)
        window = lax.dynamic_slice_in_dim(padded, start, STEPS, 1)
        term = jnp.dot(window.reshape(SAMPLES * STEPS, PCOLS).astype(jnp.float32), kernel[lag_index].astype(jnp.float32), preferred_element_type=jnp.float32)
        predicted = predicted + term.reshape(SAMPLES, STEPS, SENSORS)
    misfit = observed.astype(jnp.float32) - predicted

    def advance(history, current):
        balance = current - jnp.einsum('jsn,jmn->sm', history, coupling, precision=lax.Precision.HIGHEST)
        solved = jnp.dot(balance, diag_inverse.T, precision=lax.Precision.HIGHEST)
        history = jnp.concatenate([solved[None], history[:-1]], axis=0)
        return (history, solved)
    start_history = jnp.zeros((BAND - 1, SAMPLES, SENSORS), jnp.float32)
    final_history, solved_all = lax.scan(advance, start_history, jnp.swapaxes(misfit, 0, 1))
    return jnp.swapaxes(solved_all, 0, 1)
```

```python
import functools
import jax
import jax.numpy as jnp
from jax import lax
from jax.experimental import pallas as pl
from jax.experimental.pallas import tpu as pltpu
from jax.sharding import PartitionSpec as P

REACH = 12
LANES = 128
TILE = 256
ROWS = 8
PIECE = 4
PACE = 2
MESH = pl.DeviceIdType.MESH
F32 = jnp.float32
BF16 = jnp.bfloat16
ACROSS = (((1,), (1,)), ((), ()))


def split(value):
    high = value.astype(BF16)
    return high, (value - high.astype(F32)).astype(BF16)


def stack(value):
    return jnp.concatenate(split(value), axis=0)


def product(left, right):
    rows, width = left.shape[0], right.shape[1] // 2
    both = jnp.dot(stack(left), right, preferred_element_type=F32)
    return both[:rows, :width] + both[rows:, :width] + both[:rows, width:]


def whole_kernel(
    params_ref, map_ref, lag_ref, observed_ref, inverse_ref, coupling_ref, out_ref,
    params_in, map_in, observed_in, inverse_in, coupling_in,
    part, pair_in, partial, landed, obs, square, left_high, left_low, inverse_cat, weights,
    misfit, solved, window_0, window_1,
    load_sem, rim_send, rim_recv, pair_send, pair_recv, sum_send, sum_recv, out_send, out_recv,
    mate_send, mate_recv,
):
    windows = (window_0, window_1)
    samples, steps, cols = params_ref.shape
    lags, sensors, _ = map_ref.shape
    band = coupling_ref.shape[0]
    width = square.shape[0]
    chunks = len(windows)
    rim = REACH - 1
    me, tm = lax.axis_index("param"), lax.axis_index("tm")
    chip, core = lax.div(me, 2), lax.rem(me, 2)
    chips, planes = lax.axis_size("param") // 2, lax.axis_size("tm")
    owners = samples // (2 * chips)
    half = samples // 2
    pieces = ROWS // PIECE

    def at(other_chip, plane):
        return {"param": 2 * other_chip + core, "tm": plane}

    mate = {"param": 2 * chip + 1 - core, "tm": tm}

    def remote(source, target, send_sem, recv_sem, device):
        return pltpu.make_async_remote_copy(
            src_ref=source, dst_ref=target, send_sem=send_sem, recv_sem=recv_sem,
            device_id=device, device_id_type=MESH,
        )

    barrier = pltpu.get_barrier_semaphore()
    loads = [
        pltpu.make_async_copy(source, target, load_sem.at[i])
        for i, (source, target) in enumerate((
            (params_ref, params_in), (map_ref, map_in), (inverse_ref, inverse_in),
            (coupling_ref, coupling_in), (observed_ref, observed_in),
        ))
    ]
    for load in loads:
        load.start()
    pl.semaphore_signal(barrier, inc=1, device_id=mate, device_id_type=MESH)
    for turn in range(chips):
        other = lax.rem(chip + turn, chips)
        for hop in range(planes):
            if turn or hop:
                pl.semaphore_signal(
                    barrier, inc=1, device_id=at(other, lax.rem(tm + hop, planes)), device_id_type=MESH
                )

    misfit[...] = jnp.zeros_like(misfit)
    square[...] = jnp.zeros_like(square)

    loads[0].wait()
    turned = jnp.swapaxes(params_in[...].astype(F32), 0, 1).astype(BF16)
    for chunk, window in enumerate(windows):
        begin = max(rim - ROWS * chunk, 0)
        window[begin:] = turned[begin + ROWS * chunk - rim : ROWS * (chunk + 1)]

    @pl.when(tm == 0)
    def _():
        for chunk, window in enumerate(windows):
            if rim > ROWS * chunk:
                window[: rim - ROWS * chunk] = jnp.zeros((rim - ROWS * chunk, samples, cols), BF16)

    pl.semaphore_wait(barrier, planes * chips)

    def rim_copy(chunk):
        count = rim - ROWS * chunk
        return remote(
            windows[-1].at[pl.ds(ROWS * (chunk + 1), count)], windows[chunk].at[pl.ds(0, count)],
            rim_send.at[chunk], rim_recv.at[chunk],
            {"param": me, "tm": lax.rem(tm + 1, planes)},
        )

    @pl.when(tm < planes - 1)
    def _():
        for chunk in reversed(range(chunks)):
            rim_copy(chunk).start()

    def pair_copy(chunk):
        return remote(
            part.at[pl.ds((chunk * samples + (1 - core) * half) * ROWS, half * ROWS)], pair_in.at[chunk],
            pair_send.at[chunk], pair_recv.at[chunk], mate,
        )

    def forward(chunk):
        @pl.when(tm > 0)
        def _():
            rim_copy(chunk).wait_recv()

        total = None
        for lag in range(lags):
            start = rim - lag_ref[lag]
            left = windows[chunk][pl.ds(start, ROWS)].reshape(ROWS * samples, cols)
            term = lax.dot_general(left, map_in[lag], ACROSS, preferred_element_type=F32)
            total = term if total is None else total + term
        total = jnp.swapaxes(total.reshape(ROWS, samples, sensors), 0, 1)
        part[pl.ds(chunk * samples * ROWS, samples * ROWS), :] = total.reshape(samples * ROWS, sensors)
        pair_copy(chunk).start()

    def sum_copy(chunk, turn, owner):
        other = lax.rem(chip + turn, chips)
        return remote(
            partial.at[chunk, pl.ds((other * owners + owner) * ROWS, ROWS)],
            landed.at[tm * chunks + chunk, chip],
            sum_send.at[chunk, turn * owners + owner], sum_recv.at[tm * chunks + chunk, chip],
            at(other, owner),
        )

    def scatter(chunk):
        pair_copy(chunk).wait_recv()
        partial[chunk] = part[pl.ds((chunk * samples + core * half) * ROWS, half * ROWS), :] + pair_in[chunk]
        for owner in range(owners):
            rows = pl.ds((chip * owners + owner) * ROWS, ROWS)
            partial[chunk, rows, :] = partial[chunk, rows, :] - obs[owner, pl.ds(chunk * ROWS, ROWS), :]
        for turn in range(chips):
            for owner in range(owners):
                if turn:
                    sum_copy(chunk, turn, owner).start()
                else:
                    @pl.when(tm != owner)
                    def _():
                        sum_copy(chunk, 0, owner).start()

                    @pl.when(tm == owner)
                    def _():
                        landed[tm * chunks + chunk, chip] = partial[
                            chunk, pl.ds((chip * owners + owner) * ROWS, ROWS), :
                        ]

    def prepare():
        loads[2].wait()
        square[:sensors, :sensors] = inverse_in[...]
        whole = square[...]
        high, low = split(whole)
        left_high[...] = high
        left_low[...] = low
        high, low = split(jnp.transpose(whole))
        inverse_cat[:, :width] = high
        inverse_cat[:, width:] = low
        loads[3].wait()

    def compose(lag):
        square[:sensors, :sensors] = coupling_in[lag]
        high, low = split(square[...])
        for begin in range(0, width, TILE):
            end = min(begin + TILE, width)
            count = end - begin
            above = left_high[begin:end, :end]
            both = jnp.dot(
                jnp.concatenate([above, left_low[begin:end, :end]], axis=0), high[:end],
                preferred_element_type=F32,
            )
            rows = both[:count] + both[count:] + jnp.dot(above, low[:end], preferred_element_type=F32)
            turned = split(jnp.transpose(rows))
            place = pl.ds(pl.multiple_of(lag * width, LANES), width)
            weights[place, begin:end] = turned[0]
            weights[place, width + begin : width + end] = turned[1]

    first = jnp.where(tm == 0, 0, band)
    loads[1].wait()
    loads[4].wait()
    obs[...] = observed_in[pl.ds(core * half + chip * owners, owners)].astype(F32)

    def slot(index, carry):
        base = jnp.where(tm == 0, chunks, 0)
        for chunk in range(chunks):
            turn = first + jnp.where(tm == 0, chunk, chunks - 1 - chunk)

            @pl.when(index == turn)
            def _():
                forward(chunk)

        @pl.when(index == base)
        def _():
            prepare()

        @pl.when((index >= base) & (index < base + band))
        def _():
            compose(index - base)

        for chunk in range(chunks):
            turn = first + jnp.where(tm == 0, chunk, chunks - 1 - chunk)

            @pl.when(index == turn + 1)
            def _():
                scatter(chunk)

        return carry

    lax.fori_loop(0, chunks + band + 1, slot, 0)

    mine = core * half + chip * owners + tm

    def out_copy(piece, turn, plane):
        local = piece - plane * chunks * pieces
        return remote(
            solved.at[piece], out_ref.at[mine, local],
            out_send.at[piece, turn], out_recv.at[local, chip * owners + tm],
            at(lax.rem(chip + turn, chips), plane),
        )

    row = lax.broadcasted_iota(jnp.int32, (ROWS, width), 0)

    def advance(chunk, past):
        one, two, three = past
        plane = lax.div(chunk, chunks)
        total = None
        for turn in range(chips):
            source = lax.rem(chip + turn, chips)
            arrival = remote(
                landed.at[chunk, source], landed.at[chunk, source],
                sum_send.at[0, 0], sum_recv.at[chunk, source], mate,
            )
            if turn:
                arrival.wait_recv()
            else:
                @pl.when(plane != tm)
                def _():
                    arrival.wait_recv()
            term = landed[chunk, source]
            total = term if total is None else total + term
        misfit[:, :sensors] = -total
        base = product(misfit[...], inverse_cat[...])
        for block in range(ROWS // PACE):
            now = base if block == 0 else pltpu.roll(base, ROWS - PACE * block, 0)
            now = jnp.where(row < PACE, now, 0.0)
            carry = product(jnp.concatenate([one, two, three], axis=-1), weights[...])
            now = now - carry
            down = jnp.where(row == 1, pltpu.roll(now, 1, 0), 0.0)
            now = now - product(down, weights[:width, :])
            piece = chunk * pieces + (block * PACE) // PIECE
            begin = (block * PACE) % PIECE
            solved[piece, begin : begin + PACE, :] = now[:PACE, :sensors]
            one = jnp.where(row == 0, pltpu.roll(now, ROWS - 1, 0), 0.0)
            three = jnp.where(row == 0, pltpu.roll(two, ROWS - 1, 0), down)
            three = jnp.where(row == 1, pltpu.roll(now, 1, 0), three)
            two = now
            if begin + PACE == PIECE:
                for turn in range(chips):
                    if turn:
                        out_copy(piece, turn, plane).start()
                    else:
                        @pl.when(plane != tm)
                        def _():
                            out_copy(piece, 0, plane).start()

                        @pl.when(plane == tm)
                        def _():
                            out_ref[mine, piece - plane * chunks * pieces] = solved[piece]
        return one, two, three

    @pl.when(tm < owners)
    def _():
        nothing = jnp.zeros((ROWS, width), F32)
        lax.fori_loop(0, planes * chunks, advance, (nothing,) * 3)

    def mate_copy(piece):
        block = out_ref.at[pl.ds(core * half, half), piece]
        return remote(block, block, mate_send.at[piece], mate_recv.at[piece], mate)

    def hand(piece, carry):
        for turn in range(chips):
            source = lax.rem(chip + turn, chips)
            for owner in range(owners):
                block = out_ref.at[core * half + source * owners + owner, piece]
                arrival = remote(
                    block, block, mate_send.at[0], out_recv.at[piece, source * owners + owner], mate
                )
                if turn:
                    arrival.wait_recv()
                else:
                    @pl.when(tm != owner)
                    def _():
                        arrival.wait_recv()
        mate_copy(piece).start()
        return carry

    lax.fori_loop(0, chunks * pieces, hand, 0)

    def settle(piece, carry):
        plane = lax.div(piece, chunks * pieces)
        for turn in range(chips):
            if turn:
                out_copy(piece, turn, plane).wait_send()
            else:
                @pl.when(plane != tm)
                def _():
                    out_copy(piece, 0, plane).wait_send()
        return carry

    @pl.when(tm < owners)
    def _():
        lax.fori_loop(0, planes * chunks * pieces, settle, 0)

    @pl.when(tm < planes - 1)
    def _():
        for chunk in range(chunks):
            rim_copy(chunk).wait_send()

    for chunk in range(chunks):
        pair_copy(chunk).wait_send()
        for turn in range(chips):
            for owner in range(owners):
                if turn:
                    sum_copy(chunk, turn, owner).wait_send()
                else:
                    @pl.when(tm != owner)
                    def _():
                        sum_copy(chunk, 0, owner).wait_send()
    for piece in range(chunks * pieces):
        mate_copy(piece).wait_send()
        mate_copy(piece).wait_recv()


def per_device(params, kernel, lag_offsets, observed, diag_inverse, coupling):
    samples, steps, cols = params.shape
    lags, _, sensors = kernel.shape
    band = coupling.shape[0]
    width = -(-sensors // LANES) * LANES
    chips, planes = lax.axis_size("param") // 2, lax.axis_size("tm")
    chunks = steps // ROWS
    owners = samples // (2 * chips)
    half = samples // 2
    pieces = ROWS // PIECE
    span = REACH - 1 + ROWS
    vmem, dma = pltpu.VMEM, pltpu.SemaphoreType.DMA
    hbm = pl.BlockSpec(memory_space=pl.ANY)
    gathered = pl.pallas_call(
        whole_kernel,
        out_shape=jax.ShapeDtypeStruct((samples, steps // PIECE, PIECE, sensors), F32),
        in_specs=[hbm, hbm, pl.BlockSpec(memory_space=pltpu.SMEM), hbm, hbm, hbm],
        out_specs=pl.BlockSpec(memory_space=pltpu.VMEM),
        scratch_shapes=[
            vmem(params.shape, BF16),
            vmem((lags, sensors, cols), BF16),
            vmem(observed.shape, BF16),
            vmem(diag_inverse.shape, F32),
            vmem(coupling.shape, F32),
            vmem((samples * steps, sensors), F32),
            vmem((chunks, half * ROWS, sensors), F32),
            vmem((chunks, half * ROWS, sensors), F32),
            vmem((planes * chunks, chips, ROWS, sensors), F32),
            vmem((owners, steps, sensors), F32),
            vmem((width, width), F32),
            vmem((width, width), BF16),
            vmem((width, width), BF16),
            vmem((width, 2 * width), BF16),
            vmem((band * width, 2 * width), BF16),
            vmem((ROWS, width), F32),
            vmem((planes * chunks * pieces, PIECE, sensors), F32),
            vmem((span, samples, cols), BF16),
            vmem((span, samples, cols), BF16),
            dma((5,)),
            dma((chunks,)),
            dma((chunks,)),
            dma((chunks,)),
            dma((chunks,)),
            dma((chunks, chips * owners)),
            dma((planes * chunks, chips)),
            dma((planes * chunks * pieces, chips)),
            dma((chunks * pieces, chips * owners)),
            dma((chunks * pieces,)),
            dma((chunks * pieces,)),
        ],
        compiler_params=pltpu.CompilerParams(
            collective_id=0, has_side_effects=True, vmem_limit_bytes=48 * 2**20
        ),
    )(params, jnp.swapaxes(kernel, 1, 2), lag_offsets, observed, diag_inverse, coupling)
    return gathered.reshape(samples, steps, sensors)


def solution(mesh):
    in_specs = (P(None, "tm", "param"), P(None, "param", None), P(), P(None, "tm", None), P(), P())
    out_specs = P(None, "tm", None)
    return jax.shard_map(
        per_device, mesh=mesh, in_specs=in_specs, out_specs=out_specs, check_vma=False
    )
```

```python
import math
import jax
import jax.numpy as jnp
from jax import lax
from jax.experimental import pallas as pl
from jax.experimental.pallas import tpu as pltpu
from jax.sharding import PartitionSpec as P

REACH = 12
LANES = 128
TILE = 256
ROWS = 8
PIECE = 4
PACE = 2
LAG = 3
LEVELS = 4
MESH = pl.DeviceIdType.MESH
F32 = jnp.float32
BF16 = jnp.bfloat16
ACROSS = (((1,), (1,)), ((), ()))


def split(value):
    high = value.astype(BF16)
    return high, (value - high.astype(F32)).astype(BF16)


def stack(value):
    return jnp.concatenate(split(value), axis=0)


def product(left, right):
    rows, width = left.shape[0], right.shape[1] // 2
    both = jnp.dot(stack(left), right, preferred_element_type=F32)
    return both[:rows, :width] + both[rows:, :width] + both[:rows, width:]


def layout():
    chips = lax.axis_size("param") // 2
    depth = math.gcd(chips, LEVELS)
    return depth, chips // depth


def spill_extents():
    rim = REACH - 1
    return tuple(-(-min(rim - begin, ROWS) // PIECE) * PIECE for begin in range(0, rim, ROWS))


def whole_kernel(
    params_ref, map_ref, lag_ref, observed_ref, inverse_ref, coupling_ref, out_ref,
    params_in, map_in, observed_in, inverse_in, coupling_in,
    window, part, pair_in, partial, side_in, ready, landed, spilled, obs, square, left_high, left_low,
    inverse_cat, weights, misfit, solved,
    load_sem, pair_send, pair_recv, side_send, side_recv, sum_send, sum_recv, spill_recv,
    out_send, out_recv, over_send, over_recv, mate_send, mate_recv,
):
    samples, steps, cols = params_ref.shape
    lags, sensors, _ = map_ref.shape
    band = coupling_ref.shape[0]
    width = square.shape[0]
    chunks = steps // ROWS
    rim = REACH - 1
    spills = -(-rim // ROWS)
    extents = (ROWS,) * chunks + spill_extents()
    me, tm = lax.axis_index("param"), lax.axis_index("tm")
    depth, breadth = layout()
    core, side, level = lax.rem(me, 2), lax.rem(lax.div(me, 2), breadth), lax.div(me, 2 * breadth)
    planes = lax.axis_size("tm")
    owners = samples // (2 * depth * breadth)
    group = depth * owners
    half = samples // 2
    pieces = ROWS // PIECE

    def along(distance, plane):
        return {"param": (lax.rem(level + distance, depth) * breadth + side) * 2 + core, "tm": plane}

    def beside(distance):
        return {"param": (level * breadth + lax.rem(side + distance, breadth)) * 2 + core, "tm": tm}

    mate = {"param": me + 1 - 2 * core, "tm": tm}

    def remote(source, target, send_sem, recv_sem, device):
        return pltpu.make_async_remote_copy(
            src_ref=source, dst_ref=target, send_sem=send_sem, recv_sem=recv_sem,
            device_id=device, device_id_type=MESH,
        )

    barrier = pltpu.get_barrier_semaphore()
    loads = [
        pltpu.make_async_copy(source, target, load_sem.at[i])
        for i, (source, target) in enumerate((
            (params_ref, params_in), (map_ref, map_in), (inverse_ref, inverse_in),
            (coupling_ref, coupling_in), (observed_ref, observed_in),
        ))
    ]
    for load in loads:
        load.start()
    pl.semaphore_signal(barrier, inc=1, device_id=mate, device_id_type=MESH)
    for turn in range(1, breadth):
        pl.semaphore_signal(barrier, inc=1, device_id=beside(turn), device_id_type=MESH)
    for turn in range(depth):
        for hop in range(planes):
            if turn or hop:
                device = along(turn, lax.rem(tm + hop, planes))
                pl.semaphore_signal(barrier, inc=1, device_id=device, device_id_type=MESH)

    misfit[...] = jnp.zeros_like(misfit)
    square[...] = jnp.zeros_like(square)

    loads[0].wait()
    turned = jnp.swapaxes(params_in[...].astype(F32), 0, 1).astype(BF16)
    window[:rim] = jnp.zeros((rim, samples, cols), BF16)
    window[rim : rim + steps] = turned
    behind = window.shape[0] - rim - steps
    window[rim + steps :] = jnp.zeros((behind, samples, cols), BF16)
    for chunk, extent in enumerate(spill_extents()):
        if extent < ROWS:
            blank = jnp.zeros((planes, depth, ROWS - extent, sensors), F32)
            spilled[:, chunk, :, extent:, :] = blank
    pl.semaphore_wait(barrier, planes * depth + breadth - 1)

    def pair_copy(chunk):
        return remote(
            part.at[chunk, pl.ds((1 - core) * half, half), pl.ds(0, extents[chunk])],
            pair_in.at[chunk, :, pl.ds(0, extents[chunk])],
            pair_send.at[chunk], pair_recv.at[chunk], mate,
        )

    def forward(chunk):
        extent = extents[chunk]
        total = None
        for lag in range(lags):
            start = rim + ROWS * chunk - lag_ref[lag]
            left = window[pl.ds(start, extent)].reshape(extent * samples, cols)
            term = lax.dot_general(left, map_in[lag], ACROSS, preferred_element_type=F32)
            total = term if total is None else total + term
        part[chunk, :, :extent, :] = jnp.swapaxes(total.reshape(extent, samples, sensors), 0, 1)
        pair_copy(chunk).start()

    def side_copy(chunk, turn):
        rows = pl.ds(0, extents[chunk])
        other = lax.rem(side + turn, breadth)
        return remote(
            partial.at[chunk, pl.ds(other * group, group), rows], side_in.at[chunk, turn - 1, :, rows],
            side_send.at[chunk, turn - 1], side_recv.at[chunk, turn - 1], beside(turn),
        )

    def to_side(chunk):
        extent = extents[chunk]
        pair_copy(chunk).wait_recv()
        partial[chunk, :, :extent, :] = (
            part[chunk, pl.ds(core * half, half), :extent, :] + pair_in[chunk, :, :extent, :]
        )
        for turn in range(1, breadth):
            side_copy(chunk, turn).start()

    def sum_copy(chunk, turn, owner):
        rows = pl.ds(0, extents[chunk])
        if chunk < chunks:
            target, arrived = landed.at[tm, chunk, level], sum_recv.at[tm, chunk, level]
        else:
            target = spilled.at[tm + 1, chunk - chunks, level, rows]
            arrived = spill_recv.at[tm + 1, chunk - chunks, level]
        return remote(
            ready.at[chunk, lax.rem(level + turn, depth) * owners + owner, rows], target,
            sum_send.at[chunk, turn * owners + owner], arrived, along(turn, owner),
        )

    def to_owner(chunk):
        extent = extents[chunk]
        total = partial[chunk, pl.ds(side * group, group), :extent, :]
        for turn in range(1, breadth):
            side_copy(chunk, turn).wait_recv()
            total = total + side_in[chunk, turn - 1, :, :extent, :]
        ready[chunk, :, :extent, :] = total
        if chunk < chunks:
            for owner in range(owners):
                place = level * owners + owner
                ready[chunk, place] = ready[chunk, place] - obs[owner, chunk * ROWS : (chunk + 1) * ROWS, :]
        for turn in range(depth):
            for owner in range(owners):
                if turn:
                    sum_copy(chunk, turn, owner).start()
                else:
                    @pl.when(tm != owner)
                    def _():
                        sum_copy(chunk, 0, owner).start()

                    @pl.when(tm == owner)
                    def _():
                        own = ready[chunk, level * owners + owner, :extent, :]
                        if chunk < chunks:
                            landed[tm, chunk, level] = own
                        else:
                            spilled[tm + 1, chunk - chunks, level, :extent, :] = own

    def prepare():
        loads[2].wait()
        square[:sensors, :sensors] = inverse_in[...]
        whole = square[...]
        high, low = split(whole)
        left_high[...] = high
        left_low[...] = low
        high, low = split(jnp.transpose(whole))
        inverse_cat[:, :width] = high
        inverse_cat[:, width:] = low
        loads[3].wait()

    def compose(lag):
        square[:sensors, :sensors] = coupling_in[lag]
        high, low = split(square[...])
        for begin in range(0, width, TILE):
            end = min(begin + TILE, width)
            count = end - begin
            above = left_high[begin:end, :end]
            both = jnp.dot(
                jnp.concatenate([above, left_low[begin:end, :end]], axis=0), high[:end],
                preferred_element_type=F32,
            )
            rows = both[:count] + both[count:] + jnp.dot(above, low[:end], preferred_element_type=F32)
            turned = split(jnp.transpose(rows))
            place = pl.ds(pl.multiple_of(lag * width, LANES), width)
            weights[place, begin:end] = turned[0]
            weights[place, width + begin : width + end] = turned[1]

    loads[1].wait()
    loads[4].wait()
    obs[...] = observed_in[pl.ds(core * half + side * group + level * owners, owners)].astype(F32)

    count = len(extents)
    early = tm == 0
    first, base = jnp.where(early, 0, band), jnp.where(early, count, 0)

    def each(step):
        for chunk in range(count):
            reached = step == first + chunk
            yield chunk, reached if chunk < chunks else reached & (tm < planes - 1)

    def slot(index, carry):
        for chunk, reached in each(index):
            @pl.when(reached)
            def _():
                forward(chunk)

        @pl.when(index == base)
        def _():
            prepare()

        @pl.when((index >= base) & (index < base + band))
        def _():
            compose(index - base)

        for chunk, reached in each(index - 1):
            @pl.when(reached)
            def _():
                to_side(chunk)

        for chunk, reached in each(index - 3):
            @pl.when(reached)
            def _():
                to_owner(chunk)

        return carry

    lax.fori_loop(0, count + band + 3, slot, 0)

    mine = core * half + side * group + level * owners + tm

    def out_copy(piece, turn, plane):
        local = piece - plane * chunks * pieces
        return remote(
            solved.at[piece], out_ref.at[mine, local],
            out_send.at[piece, turn], out_recv.at[local, level * owners + tm], along(turn, plane),
        )

    def over_copy(piece, turn):
        block = out_ref.at[pl.ds(core * half + side * group, group), piece]
        return remote(
            block, block, over_send.at[piece, turn - 1], over_recv.at[piece, turn - 1], beside(turn)
        )

    def hand_over(piece):
        for turn in range(depth):
            source = lax.rem(level + turn, depth)
            for owner in range(owners):
                block = out_ref.at[core * half + side * group + source * owners + owner, piece]
                arrival = remote(
                    block, block, mate_send.at[0], out_recv.at[piece, source * owners + owner], mate
                )
                if turn:
                    arrival.wait_recv()
                else:
                    @pl.when(tm != owner)
                    def _():
                        arrival.wait_recv()
        for turn in range(1, breadth):
            over_copy(piece, turn).start()

    row = lax.broadcasted_iota(jnp.int32, (ROWS, width), 0)

    def advance(chunk, past):
        one, two, three = past
        plane = lax.div(chunk, chunks)
        local = lax.rem(chunk, chunks)

        def collect(buffer, semaphores, expected, origin):
            total = None
            for turn in range(depth):
                source = lax.rem(level + turn, depth)
                place = buffer.at[plane, local, source, pl.ds(0, expected)]
                arrival = remote(place, place, sum_send.at[0, 0], semaphores.at[plane, local, source], mate)
                if turn:
                    arrival.wait_recv()
                else:
                    @pl.when(origin != tm)
                    def _():
                        arrival.wait_recv()
                term = buffer[plane, local, source]
                total = term if total is None else total + term
            return total

        misfit[:, :sensors] = -collect(landed, sum_recv, ROWS, plane)
        for spill, extent in enumerate(spill_extents()):
            @pl.when((plane > 0) & (local == spill))
            def _():
                misfit[:, :sensors] = misfit[:, :sensors] - collect(spilled, spill_recv, extent, plane - 1)

        base = product(misfit[...], inverse_cat[...])
        for block in range(ROWS // PACE):
            now = base if block == 0 else pltpu.roll(base, ROWS - PACE * block, 0)
            now = jnp.where(row < PACE, now, 0.0)
            carry = product(jnp.concatenate([one, two, three], axis=-1), weights[...])
            now = now - carry
            down = jnp.where(row == 1, pltpu.roll(now, 1, 0), 0.0)
            now = now - product(down, weights[:width, :])
            piece = chunk * pieces + (block * PACE) // PIECE
            begin = (block * PACE) % PIECE
            solved[piece, begin : begin + PACE, :] = now[:PACE, :sensors]
            one = jnp.where(row == 0, pltpu.roll(now, ROWS - 1, 0), 0.0)
            three = jnp.where(row == 0, pltpu.roll(two, ROWS - 1, 0), down)
            three = jnp.where(row == 1, pltpu.roll(now, 1, 0), three)
            two = now
            if begin + PACE == PIECE:
                for turn in range(depth):
                    if turn:
                        out_copy(piece, turn, plane).start()
                    else:
                        @pl.when(plane != tm)
                        def _():
                            out_copy(piece, 0, plane).start()

                        @pl.when(plane == tm)
                        def _():
                            out_ref[mine, piece - plane * chunks * pieces] = solved[piece]

                older = piece - LAG - tm * chunks * pieces

                @pl.when((older >= 0) & (older < chunks * pieces))
                def _():
                    hand_over(older)
        return one, two, three

    @pl.when(tm < owners)
    def _():
        nothing = jnp.zeros((ROWS, width), F32)
        lax.fori_loop(0, planes * chunks, advance, (nothing,) * 3)

    def mate_copy(piece):
        block = out_ref.at[pl.ds(core * half, half), piece]
        return remote(block, block, mate_send.at[piece], mate_recv.at[piece], mate)

    done = jnp.where(tm < owners, jnp.clip((planes - tm) * chunks * pieces - LAG, 0, chunks * pieces), 0)

    def finish(step, carry):
        @pl.when((step >= done) & (step < chunks * pieces))
        def _():
            hand_over(step)

        @pl.when(step > 0)
        def _():
            piece = step - 1
            for turn in range(1, breadth):
                over_copy(piece, turn).wait_recv()
            mate_copy(piece).start()

        return carry

    lax.fori_loop(0, chunks * pieces + 1, finish, 0)

    def settle(piece, carry):
        plane = lax.div(piece, chunks * pieces)
        for turn in range(depth):
            if turn:
                out_copy(piece, turn, plane).wait_send()
            else:
                @pl.when(plane != tm)
                def _():
                    out_copy(piece, 0, plane).wait_send()
        return carry

    @pl.when(tm < owners)
    def _():
        lax.fori_loop(0, planes * chunks * pieces, settle, 0)

    def release(chunk):
        pair_copy(chunk).wait_send()
        for turn in range(1, breadth):
            side_copy(chunk, turn).wait_send()
        for turn in range(depth):
            for owner in range(owners):
                if turn:
                    sum_copy(chunk, turn, owner).wait_send()
                else:
                    @pl.when(tm != owner)
                    def _():
                        sum_copy(chunk, 0, owner).wait_send()

    for chunk in range(count):
        if chunk < chunks:
            release(chunk)
        else:
            @pl.when(tm < planes - 1)
            def _():
                release(chunk)
    for piece in range(chunks * pieces):
        for turn in range(1, breadth):
            over_copy(piece, turn).wait_send()
        mate_copy(piece).wait_send()
        mate_copy(piece).wait_recv()


def per_device(params, kernel, lag_offsets, observed, diag_inverse, coupling):
    samples, steps, cols = params.shape
    lags, _, sensors = kernel.shape
    band = coupling.shape[0]
    width = -(-sensors // LANES) * LANES
    depth, breadth = layout()
    planes = lax.axis_size("tm")
    chunks = steps // ROWS
    owners = samples // (2 * depth * breadth)
    group = depth * owners
    half = samples // 2
    pieces = ROWS // PIECE
    spills = len(spill_extents())
    vmem, dma = pltpu.VMEM, pltpu.SemaphoreType.DMA
    hbm = pl.BlockSpec(memory_space=pl.ANY)
    gathered = pl.pallas_call(
        whole_kernel,
        out_shape=jax.ShapeDtypeStruct((samples, steps // PIECE, PIECE, sensors), F32),
        in_specs=[hbm, hbm, pl.BlockSpec(memory_space=pltpu.SMEM), hbm, hbm, hbm],
        out_specs=pl.BlockSpec(memory_space=pltpu.VMEM),
        scratch_shapes=[
            vmem(params.shape, BF16),
            vmem((lags, sensors, cols), BF16),
            vmem(observed.shape, BF16),
            vmem(diag_inverse.shape, F32),
            vmem(coupling.shape, F32),
            vmem((REACH - 1 + (chunks + spills) * ROWS, samples, cols), BF16),
            vmem((chunks + spills, samples, ROWS, sensors), F32),
            vmem((chunks + spills, half, ROWS, sensors), F32),
            vmem((chunks + spills, half, ROWS, sensors), F32),
            vmem((chunks + spills, breadth - 1, group, ROWS, sensors), F32),
            vmem((chunks + spills, group, ROWS, sensors), F32),
            vmem((planes, chunks, depth, ROWS, sensors), F32),
            vmem((planes, spills, depth, ROWS, sensors), F32),
            vmem((owners, steps, sensors), F32),
            vmem((width, width), F32),
            vmem((width, width), BF16),
            vmem((width, width), BF16),
            vmem((width, 2 * width), BF16),
            vmem((band * width, 2 * width), BF16),
            vmem((ROWS, width), F32),
            vmem((planes * chunks * pieces, PIECE, sensors), F32),
            dma((5,)),
            dma((chunks + spills,)),
            dma((chunks + spills,)),
            dma((chunks + spills, breadth - 1)),
            dma((chunks + spills, breadth - 1)),
            dma((chunks + spills, group)),
            dma((planes, chunks, depth)),
            dma((planes, spills, depth)),
            dma((planes * chunks * pieces, depth)),
            dma((chunks * pieces, group)),
            dma((chunks * pieces, breadth - 1)),
            dma((chunks * pieces, breadth - 1)),
            dma((chunks * pieces,)),
            dma((chunks * pieces,)),
        ],
        compiler_params=pltpu.CompilerParams(
            collective_id=0, has_side_effects=True, vmem_limit_bytes=60 * 2**20
        ),
    )(params, jnp.swapaxes(kernel, 1, 2), lag_offsets, observed, diag_inverse, coupling)
    return gathered.reshape(samples, steps, sensors)


def solution(mesh):
    in_specs = (P(None, "tm", "param"), P(None, "param", None), P(), P(None, "tm", None), P(), P())
    out_specs = P(None, "tm", None)
    return jax.shard_map(
        per_device, mesh=mesh, in_specs=in_specs, out_specs=out_specs, check_vma=False
    )
```

```python
import math
import jax
import jax.numpy as jnp
from jax import lax
from jax.experimental import pallas as pl
from jax.experimental.pallas import tpu as pltpu
from jax.sharding import PartitionSpec as P

REACH = 12
LANES = 128
TILE = 256
ROWS = 8
PIECE = 4
PACE = 2
SPAN = 4
LAG = 3
LEVELS = 4
MESH = pl.DeviceIdType.MESH
F32 = jnp.float32
BF16 = jnp.bfloat16
ACROSS = (((1,), (1,)), ((), ()))


def split(value):
    high = value.astype(BF16)
    return high, (value - high.astype(F32)).astype(BF16)


def stack(value):
    return jnp.concatenate(split(value), axis=0)


def product(left, right):
    rows, width = left.shape[0], right.shape[1] // 2
    both = jnp.dot(stack(left), right, preferred_element_type=F32)
    return both[:rows, :width] + both[rows:, :width] + both[:rows, width:]


def layout():
    chips = lax.axis_size("param") // 2
    depth = math.gcd(chips, LEVELS)
    return depth, chips // depth


def spill_extents():
    rim = REACH - 1
    return tuple(-(-min(rim - begin, ROWS) // PIECE) * PIECE for begin in range(0, rim, ROWS))


def whole_kernel(
    params_ref, map_ref, lag_ref, observed_ref, inverse_ref, coupling_ref, out_ref,
    params_in, map_in, observed_in, inverse_in, coupling_in,
    window, part, pair_in, partial, side_in, ready, landed, spilled, obs, square, left_high, left_low,
    inverse_cat, weights, misfit, solved,
    load_sem, pair_send, pair_recv, side_send, side_recv, sum_send, sum_recv, spill_recv,
    out_send, out_recv, last_send, last_recv, over_send, over_recv, mate_send, mate_recv,
):
    samples, steps, cols = params_ref.shape
    lags, sensors, _ = map_ref.shape
    band = coupling_ref.shape[0]
    width = square.shape[0]
    chunks = steps // ROWS
    rim = REACH - 1
    spills = -(-rim // ROWS)
    extents = (ROWS,) * chunks + spill_extents()
    me, tm = lax.axis_index("param"), lax.axis_index("tm")
    depth, breadth = layout()
    core, side, level = lax.rem(me, 2), lax.rem(lax.div(me, 2), breadth), lax.div(me, 2 * breadth)
    planes = lax.axis_size("tm")
    share = samples // (2 * depth * breadth)
    group = depth * share
    solver = tm == planes - 1
    half = samples // 2
    pieces = ROWS // PIECE

    def along(distance, plane, turn=0):
        other = lax.rem(level + distance, depth) * breadth + lax.rem(side + turn, breadth)
        return {"param": other * 2 + core, "tm": plane}

    def beside(distance):
        return {"param": (level * breadth + lax.rem(side + distance, breadth)) * 2 + core, "tm": tm}

    mate = {"param": me + 1 - 2 * core, "tm": tm}

    def remote(source, target, send_sem, recv_sem, device):
        return pltpu.make_async_remote_copy(
            src_ref=source, dst_ref=target, send_sem=send_sem, recv_sem=recv_sem,
            device_id=device, device_id_type=MESH,
        )

    barrier = pltpu.get_barrier_semaphore()
    loads = [
        pltpu.make_async_copy(source, target, load_sem.at[i])
        for i, (source, target) in enumerate((
            (params_ref, params_in), (map_ref, map_in), (observed_ref, observed_in),
            (inverse_ref, inverse_in), (coupling_ref, coupling_in),
        ))
    ]
    params_load, map_load, observed_load, inverse_load, coupling_load = loads
    for load in loads:
        load.start()
    pl.semaphore_signal(barrier, inc=1, device_id=mate, device_id_type=MESH)
    for turn in range(breadth):
        for distance in range(depth):
            for hop in range(planes):
                if turn or distance or hop:
                    device = along(distance, lax.rem(tm + hop, planes), turn)
                    pl.semaphore_signal(barrier, inc=1, device_id=device, device_id_type=MESH)

    misfit[...] = jnp.zeros_like(misfit)
    square[...] = jnp.zeros_like(square)

    params_load.wait()
    turned = jnp.swapaxes(params_in[...].astype(F32), 0, 1).astype(BF16)
    window[:rim] = jnp.zeros((rim, samples, cols), BF16)
    window[rim : rim + steps] = turned
    behind = window.shape[0] - rim - steps
    window[rim + steps :] = jnp.zeros((behind, samples, cols), BF16)
    for chunk, extent in enumerate(spill_extents()):
        if extent < ROWS:
            blank = jnp.zeros((planes, depth, share, ROWS - extent, sensors), F32)
            spilled[:, chunk, :, :, extent:, :] = blank
    pl.semaphore_wait(barrier, planes * depth * breadth)

    def pair_copy(chunk):
        return remote(
            part.at[chunk, pl.ds((1 - core) * half, half), pl.ds(0, extents[chunk])],
            pair_in.at[chunk, :, pl.ds(0, extents[chunk])],
            pair_send.at[chunk], pair_recv.at[chunk], mate,
        )

    def forward(chunk):
        extent = extents[chunk]
        total = None
        for lag in range(lags):
            start = rim + ROWS * chunk - lag_ref[lag]
            left = window[pl.ds(start, extent)].reshape(extent * samples, cols)
            term = lax.dot_general(left, map_in[lag], ACROSS, preferred_element_type=F32)
            total = term if total is None else total + term
        part[chunk, :, :extent, :] = jnp.swapaxes(total.reshape(extent, samples, sensors), 0, 1)
        pair_copy(chunk).start()

    def side_copy(chunk, turn):
        rows = pl.ds(0, extents[chunk])
        other = lax.rem(side + turn, breadth)
        return remote(
            partial.at[chunk, pl.ds(other * group, group), rows], side_in.at[chunk, turn - 1, :, rows],
            side_send.at[chunk, turn - 1], side_recv.at[chunk, turn - 1], beside(turn),
        )

    def to_side(chunk):
        extent = extents[chunk]
        pair_copy(chunk).wait_recv()
        partial[chunk, :, :extent, :] = (
            part[chunk, pl.ds(core * half, half), :extent, :] + pair_in[chunk, :, :extent, :]
        )
        for turn in range(1, breadth):
            side_copy(chunk, turn).start()

    def sum_copy(chunk, turn):
        rows = pl.ds(0, extents[chunk])
        if chunk < chunks:
            target, arrived = landed.at[tm, chunk, level], sum_recv.at[tm, chunk, level]
        else:
            target = spilled.at[tm + 1, chunk - chunks, level, :, rows]
            arrived = spill_recv.at[tm + 1, chunk - chunks, level]
        return remote(
            ready.at[chunk, pl.ds(lax.rem(level + turn, depth) * share, share), rows], target,
            sum_send.at[chunk, turn], arrived, along(turn, planes - 1),
        )

    def to_owner(chunk):
        extent = extents[chunk]
        total = partial[chunk, pl.ds(side * group, group), :extent, :]
        for turn in range(1, breadth):
            side_copy(chunk, turn).wait_recv()
            total = total + side_in[chunk, turn - 1, :, :extent, :]
        ready[chunk, :, :extent, :] = total
        if chunk < chunks:
            own = pl.ds(level * share, share)
            ready[chunk, own] = ready[chunk, own] - obs[:, chunk * ROWS : (chunk + 1) * ROWS, :]
        for turn in range(1, depth):
            sum_copy(chunk, turn).start()

        @pl.when(jnp.logical_not(solver))
        def _():
            sum_copy(chunk, 0).start()

        if chunk < chunks:
            @pl.when(solver)
            def _():
                landed[tm, chunk, level] = ready[chunk, pl.ds(level * share, share)]

    def prepare():
        inverse_load.wait()
        square[:sensors, :sensors] = inverse_in[...]
        whole = square[...]
        high, low = split(whole)
        left_high[...] = high
        left_low[...] = low
        high, low = split(jnp.transpose(whole))
        inverse_cat[:, :width] = high
        inverse_cat[:, width:] = low
        coupling_load.wait()

    def compose(lag):
        square[:sensors, :sensors] = coupling_in[lag]
        high, low = split(square[...])
        for begin in range(0, width, TILE):
            end = min(begin + TILE, width)
            count = end - begin
            above = left_high[begin:end, :end]
            both = jnp.dot(
                jnp.concatenate([above, left_low[begin:end, :end]], axis=0), high[:end],
                preferred_element_type=F32,
            )
            rows = both[:count] + both[count:] + jnp.dot(above, low[:end], preferred_element_type=F32)
            turned = split(jnp.transpose(rows))
            place = pl.ds(pl.multiple_of(lag * width, LANES), width)
            weights[place, begin:end] = turned[0]
            weights[place, width + begin : width + end] = turned[1]

    map_load.wait()
    observed_load.wait()
    obs[...] = observed_in[pl.ds(core * half + side * group + level * share, share)].astype(F32)

    count = len(extents)
    soon, later = jnp.where(solver, 1, 0), jnp.where(solver, 3, 1)

    def when(step, act):
        for chunk in range(count):
            reached = step == chunk

            @pl.when(reached if chunk < chunks else reached & jnp.logical_not(solver))
            def _():
                act(chunk)

    def slot(index, carry):
        when(index, forward)

        @pl.when(solver & (index == chunks))
        def _():
            prepare()

        @pl.when(solver & (index >= chunks) & (index < chunks + band))
        def _():
            compose(index - chunks)

        when(index - soon, to_side)
        when(index - later, to_owner)
        return carry

    lax.fori_loop(0, jnp.where(solver, chunks + max(band, 3), count + 1), slot, 0)

    @pl.when(jnp.logical_not(solver))
    def _():
        inverse_load.wait()
        coupling_load.wait()

    mine = pl.ds(core * half + side * group + level * share, share)
    last = planes * chunks * pieces - 1

    def out_copy(piece, turn, plane):
        local = piece - plane * chunks * pieces
        return remote(
            solved.at[piece], out_ref.at[mine, local],
            out_send.at[piece, turn], out_recv.at[local, level], along(turn, plane),
        )

    def last_copy(turn, other):
        return remote(
            solved.at[last], out_ref.at[mine, chunks * pieces - 1],
            last_send.at[turn, other - 1], last_recv.at[other - 1, level], along(turn, planes - 1, other),
        )

    def straight(piece):
        return solver & (piece == chunks * pieces - 1)

    def over_copy(piece, turn):
        block = out_ref.at[pl.ds(core * half + side * group, group), piece]
        return remote(
            block, block, over_send.at[piece, turn - 1], over_recv.at[piece, turn - 1], beside(turn)
        )

    def hand_over(piece):
        def block(turn, distance):
            first = core * half + lax.rem(side + turn, breadth) * group + lax.rem(level + distance, depth) * share
            return out_ref.at[pl.ds(first, share), piece]

        def arrival(source, semaphore):
            remote(source, source, mate_send.at[0], semaphore, mate).wait_recv()

        for distance in range(depth):
            source = block(0, distance)
            semaphore = out_recv.at[piece, lax.rem(level + distance, depth)]
            if distance:
                arrival(source, semaphore)
            else:
                @pl.when(jnp.logical_not(solver))
                def _():
                    arrival(source, semaphore)

        @pl.when(straight(piece))
        def _():
            for turn in range(1, breadth):
                for distance in range(depth):
                    semaphore = last_recv.at[breadth - turn - 1, lax.rem(level + distance, depth)]
                    arrival(block(turn, distance), semaphore)

        @pl.when(jnp.logical_not(straight(piece)))
        def _():
            for turn in range(1, breadth):
                over_copy(piece, turn).start()

    row = lax.broadcasted_iota(jnp.int32, (ROWS, width), 0)
    inner = lax.rem(row, SPAN)

    def advance(chunk, past):
        one, two, three = past
        plane = lax.div(chunk, chunks)
        local = lax.rem(chunk, chunks)

        def collect(buffer, semaphores, expected, origin):
            total = None
            for turn in range(depth):
                source = lax.rem(level + turn, depth)
                place = buffer.at[plane, local, source, :, pl.ds(0, expected)]
                arrival = remote(place, place, sum_send.at[0, 0], semaphores.at[plane, local, source], mate)
                if turn:
                    arrival.wait_recv()
                else:
                    @pl.when(origin != planes - 1)
                    def _():
                        arrival.wait_recv()
                term = buffer[plane, local, source]
                total = term if total is None else total + term
            return total

        misfit[:, :, :sensors] = -collect(landed, sum_recv, ROWS, plane)
        for spill, extent in enumerate(spill_extents()):
            @pl.when((plane > 0) & (local == spill))
            def _():
                more = collect(spilled, spill_recv, extent, plane - 1)
                misfit[:, :, :sensors] = misfit[:, :, :sensors] - more

        base = product(misfit[...].reshape(share * ROWS, width), inverse_cat[...])
        for block in range(ROWS // PACE):
            now = jnp.zeros((ROWS, width), F32)
            for sample in range(share):
                rows = base[sample * ROWS : (sample + 1) * ROWS]
                shift = (sample * SPAN - PACE * block) % ROWS
                rows = pltpu.roll(rows, shift, 0) if shift else rows
                begin = sample * SPAN
                now = jnp.where((row >= begin) & (row < begin + PACE), rows, now)
            carry = product(jnp.concatenate([one, two, three], axis=-1), weights[...])
            now = now - carry
            down = jnp.where(inner == 1, pltpu.roll(now, 1, 0), 0.0)
            now = now - product(down, weights[:width, :])
            piece = chunk * pieces + (block * PACE) // PIECE
            begin = (block * PACE) % PIECE
            for sample in range(share):
                rows = now[sample * SPAN : sample * SPAN + PACE, :sensors]
                solved[piece, sample, begin : begin + PACE, :] = rows
            one = jnp.where(inner == 0, pltpu.roll(now, ROWS - 1, 0), 0.0)
            three = jnp.where(inner == 0, pltpu.roll(two, ROWS - 1, 0), down)
            three = jnp.where(inner == 1, pltpu.roll(now, 1, 0), three)
            two = now
            if begin + PACE == PIECE:
                for turn in range(depth):
                    if turn:
                        out_copy(piece, turn, plane).start()
                    else:
                        @pl.when(plane != planes - 1)
                        def _():
                            out_copy(piece, 0, plane).start()

                        @pl.when(plane == planes - 1)
                        def _():
                            out_ref[mine, piece - plane * chunks * pieces] = solved[piece]

                @pl.when(piece == last)
                def _():
                    for turn in range(depth):
                        for other in range(1, breadth):
                            last_copy(turn, other).start()

                older = piece - LAG - tm * chunks * pieces

                @pl.when((older >= 0) & (older < chunks * pieces))
                def _():
                    hand_over(older)
        return one, two, three

    @pl.when(solver)
    def _():
        nothing = jnp.zeros((ROWS, width), F32)
        lax.fori_loop(0, planes * chunks, advance, (nothing,) * 3)

    def mate_copy(piece):
        block = out_ref.at[pl.ds(core * half, half), piece]
        return remote(block, block, mate_send.at[piece], mate_recv.at[piece], mate)

    done = jnp.where(solver, max(chunks * pieces - LAG, 0), 0)

    def finish(step, carry):
        @pl.when((step >= done) & (step < chunks * pieces))
        def _():
            hand_over(step)

        @pl.when(step > 0)
        def _():
            piece = step - 1

            @pl.when(jnp.logical_not(straight(piece)))
            def _():
                for turn in range(1, breadth):
                    over_copy(piece, turn).wait_recv()

            mate_copy(piece).start()

        return carry

    lax.fori_loop(0, chunks * pieces + 1, finish, 0)

    def settle(piece, carry):
        plane = lax.div(piece, chunks * pieces)
        for turn in range(depth):
            if turn:
                out_copy(piece, turn, plane).wait_send()
            else:
                @pl.when(plane != planes - 1)
                def _():
                    out_copy(piece, 0, plane).wait_send()
        return carry

    @pl.when(solver)
    def _():
        lax.fori_loop(0, planes * chunks * pieces, settle, 0)
        for turn in range(depth):
            for other in range(1, breadth):
                last_copy(turn, other).wait_send()

    def release(chunk):
        pair_copy(chunk).wait_send()
        for turn in range(1, breadth):
            side_copy(chunk, turn).wait_send()
        for turn in range(1, depth):
            sum_copy(chunk, turn).wait_send()

        @pl.when(jnp.logical_not(solver))
        def _():
            sum_copy(chunk, 0).wait_send()

    for chunk in range(count):
        if chunk < chunks:
            release(chunk)
        else:
            @pl.when(tm < planes - 1)
            def _():
                release(chunk)
    for piece in range(chunks * pieces):
        @pl.when(jnp.logical_not(straight(piece)))
        def _():
            for turn in range(1, breadth):
                over_copy(piece, turn).wait_send()

        mate_copy(piece).wait_send()
        mate_copy(piece).wait_recv()


def per_device(params, kernel, lag_offsets, observed, diag_inverse, coupling):
    samples, steps, cols = params.shape
    lags, _, sensors = kernel.shape
    band = coupling.shape[0]
    width = -(-sensors // LANES) * LANES
    depth, breadth = layout()
    planes = lax.axis_size("tm")
    chunks = steps // ROWS
    share = samples // (2 * depth * breadth)
    group = depth * share
    half = samples // 2
    pieces = ROWS // PIECE
    spills = len(spill_extents())
    vmem, dma = pltpu.VMEM, pltpu.SemaphoreType.DMA
    hbm = pl.BlockSpec(memory_space=pl.ANY)
    gathered = pl.pallas_call(
        whole_kernel,
        out_shape=jax.ShapeDtypeStruct((samples, steps // PIECE, PIECE, sensors), F32),
        in_specs=[hbm, hbm, pl.BlockSpec(memory_space=pltpu.SMEM), hbm, hbm, hbm],
        out_specs=pl.BlockSpec(memory_space=pltpu.VMEM),
        scratch_shapes=[
            vmem(params.shape, BF16),
            vmem((lags, sensors, cols), BF16),
            vmem(observed.shape, BF16),
            vmem(diag_inverse.shape, F32),
            vmem(coupling.shape, F32),
            vmem((REACH - 1 + (chunks + spills) * ROWS, samples, cols), BF16),
            vmem((chunks + spills, samples, ROWS, sensors), F32),
            vmem((chunks + spills, half, ROWS, sensors), F32),
            vmem((chunks + spills, half, ROWS, sensors), F32),
            vmem((chunks + spills, breadth - 1, group, ROWS, sensors), F32),
            vmem((chunks + spills, group, ROWS, sensors), F32),
            vmem((planes, chunks, depth, share, ROWS, sensors), F32),
            vmem((planes, spills, depth, share, ROWS, sensors), F32),
            vmem((share, steps, sensors), F32),
            vmem((width, width), F32),
            vmem((width, width), BF16),
            vmem((width, width), BF16),
            vmem((width, 2 * width), BF16),
            vmem((band * width, 2 * width), BF16),
            vmem((share, ROWS, width), F32),
            vmem((planes * chunks * pieces, share, PIECE, sensors), F32),
            dma((5,)),
            dma((chunks + spills,)),
            dma((chunks + spills,)),
            dma((chunks + spills, breadth - 1)),
            dma((chunks + spills, breadth - 1)),
            dma((chunks + spills, depth)),
            dma((planes, chunks, depth)),
            dma((planes, spills, depth)),
            dma((planes * chunks * pieces, depth)),
            dma((chunks * pieces, depth)),
            dma((depth, breadth - 1)),
            dma((breadth - 1, depth)),
            dma((chunks * pieces, breadth - 1)),
            dma((chunks * pieces, breadth - 1)),
            dma((chunks * pieces,)),
            dma((chunks * pieces,)),
        ],
        compiler_params=pltpu.CompilerParams(
            collective_id=0, has_side_effects=True, vmem_limit_bytes=60 * 2**20
        ),
    )(params, jnp.swapaxes(kernel, 1, 2), lag_offsets, observed, diag_inverse, coupling)
    return gathered.reshape(samples, steps, sensors)


def solution(mesh):
    in_specs = (P(None, "tm", "param"), P(None, "param", None), P(), P(None, "tm", None), P(), P())
    out_specs = P(None, "tm", None)
    return jax.shard_map(
        per_device, mesh=mesh, in_specs=in_specs, out_specs=out_specs, check_vma=False
    )
```

```python
import math
import jax
import jax.numpy as jnp
from jax import lax
from jax.experimental import pallas as pl
from jax.experimental.pallas import tpu as pltpu
from jax.sharding import PartitionSpec as P

REACH = 12
LANES = 128
TILE = 256
ROWS = 8
PIECE = 4
PACE = 2
SPAN = 4
LAG = 2
LEVELS = 4
MESH = pl.DeviceIdType.MESH
F32 = jnp.float32
BF16 = jnp.bfloat16
ACROSS = (((1,), (1,)), ((), ()))


def split(value):
    high = value.astype(BF16)
    return high, (value - high.astype(F32)).astype(BF16)


def stack(value):
    return jnp.concatenate(split(value), axis=0)


def product(left, right):
    rows, width = left.shape[0], right.shape[1] // 2
    both = jnp.dot(stack(left), right, preferred_element_type=F32)
    return both[:rows, :width] + both[rows:, :width] + both[:rows, width:]


def layout():
    chips = lax.axis_size("param") // 2
    depth = math.gcd(chips, LEVELS)
    return depth, chips // depth


def spill_extents():
    rim = REACH - 1
    return tuple(-(-min(rim - begin, ROWS) // PIECE) * PIECE for begin in range(0, rim, ROWS))


def whole_kernel(
    params_ref, map_ref, lag_ref, observed_ref, inverse_ref, coupling_ref, out_ref,
    params_in, map_in, observed_in, inverse_in, coupling_in,
    window, part, pair_in, partial, side_in, ready, landed, spilled, obs, square, left_high, left_low,
    inverse_cat, weights, misfit, solved,
    load_sem, pair_send, pair_recv, side_send, side_recv, sum_send, sum_recv, spill_recv,
    out_send, out_recv, last_send, last_recv, over_send, over_recv, mate_send, mate_recv,
):
    samples, steps, cols = params_ref.shape
    lags, sensors, _ = map_ref.shape
    band = coupling_ref.shape[0]
    width = square.shape[0]
    chunks = steps // ROWS
    rim = REACH - 1
    spills = -(-rim // ROWS)
    extents = (ROWS,) * chunks + spill_extents()
    me, tm = lax.axis_index("param"), lax.axis_index("tm")
    depth, breadth = layout()
    core, side, level = lax.rem(me, 2), lax.rem(lax.div(me, 2), breadth), lax.div(me, 2 * breadth)
    planes = lax.axis_size("tm")
    share = samples // (2 * depth * breadth)
    group = depth * share
    solver = tm == planes - 1
    half = samples // 2
    pieces = ROWS // PIECE

    def along(distance, plane, turn=0):
        other = lax.rem(level + distance, depth) * breadth + lax.rem(side + turn, breadth)
        return {"param": other * 2 + core, "tm": plane}

    def beside(distance):
        return {"param": (level * breadth + lax.rem(side + distance, breadth)) * 2 + core, "tm": tm}

    mate = {"param": me + 1 - 2 * core, "tm": tm}

    def remote(source, target, send_sem, recv_sem, device):
        return pltpu.make_async_remote_copy(
            src_ref=source, dst_ref=target, send_sem=send_sem, recv_sem=recv_sem,
            device_id=device, device_id_type=MESH,
        )

    barrier = pltpu.get_barrier_semaphore()
    loads = [
        pltpu.make_async_copy(source, target, load_sem.at[i])
        for i, (source, target) in enumerate((
            (params_ref, params_in), (map_ref, map_in), (observed_ref, observed_in),
            (inverse_ref, inverse_in), (coupling_ref, coupling_in),
        ))
    ]
    params_load, map_load, observed_load, inverse_load, coupling_load = loads
    for load in loads[:3]:
        load.start()

    @pl.when(solver)
    def _():
        inverse_load.start()
        coupling_load.start()

    pl.semaphore_signal(barrier, inc=1, device_id=mate, device_id_type=MESH)
    for turn in range(breadth):
        for distance in range(depth):
            for hop in range(planes):
                if turn or distance or hop:
                    device = along(distance, lax.rem(tm + hop, planes), turn)
                    pl.semaphore_signal(barrier, inc=1, device_id=device, device_id_type=MESH)

    misfit[...] = jnp.zeros_like(misfit)
    square[...] = jnp.zeros_like(square)

    params_load.wait()
    turned = jnp.swapaxes(params_in[...].astype(F32), 0, 1).astype(BF16)
    window[:rim] = jnp.zeros((rim, samples, cols), BF16)
    window[rim : rim + steps] = turned
    behind = window.shape[0] - rim - steps
    window[rim + steps :] = jnp.zeros((behind, samples, cols), BF16)
    for chunk, extent in enumerate(spill_extents()):
        if extent < ROWS:
            blank = jnp.zeros((planes, depth, share, ROWS - extent, sensors), F32)
            spilled[:, chunk, :, :, extent:, :] = blank
    pl.semaphore_wait(barrier, planes * depth * breadth)

    def pair_copy(chunk):
        return remote(
            part.at[chunk, pl.ds((1 - core) * half, half), pl.ds(0, extents[chunk])],
            pair_in.at[chunk, :, pl.ds(0, extents[chunk])],
            pair_send.at[chunk], pair_recv.at[chunk], mate,
        )

    def forward(chunk):
        extent = extents[chunk]
        total = None
        for lag in range(lags):
            start = rim + ROWS * chunk - lag_ref[lag]
            left = window[pl.ds(start, extent)].reshape(extent * samples, cols)
            term = lax.dot_general(left, map_in[lag], ACROSS, preferred_element_type=F32)
            total = term if total is None else total + term
        part[chunk, :, :extent, :] = jnp.swapaxes(total.reshape(extent, samples, sensors), 0, 1)
        pair_copy(chunk).start()

    def side_copy(chunk, turn):
        rows = pl.ds(0, extents[chunk])
        other = lax.rem(side + turn, breadth)
        return remote(
            partial.at[chunk, pl.ds(other * group, group), rows], side_in.at[chunk, turn - 1, :, rows],
            side_send.at[chunk, turn - 1], side_recv.at[chunk, turn - 1], beside(turn),
        )

    def to_side(chunk):
        extent = extents[chunk]
        pair_copy(chunk).wait_recv()
        partial[chunk, :, :extent, :] = (
            part[chunk, pl.ds(core * half, half), :extent, :] + pair_in[chunk, :, :extent, :]
        )
        for turn in range(1, breadth):
            side_copy(chunk, turn).start()

    def sum_copy(chunk, turn):
        rows = pl.ds(0, extents[chunk])
        if chunk < chunks:
            target, arrived = landed.at[tm, chunk, level], sum_recv.at[tm, chunk, level]
        else:
            target = spilled.at[tm + 1, chunk - chunks, level, :, rows]
            arrived = spill_recv.at[tm + 1, chunk - chunks, level]
        return remote(
            ready.at[chunk, pl.ds(lax.rem(level + turn, depth) * share, share), rows], target,
            sum_send.at[chunk, turn], arrived, along(turn, planes - 1),
        )

    def to_owner(chunk):
        extent = extents[chunk]
        total = partial[chunk, pl.ds(side * group, group), :extent, :]
        for turn in range(1, breadth):
            side_copy(chunk, turn).wait_recv()
            total = total + side_in[chunk, turn - 1, :, :extent, :]
        ready[chunk, :, :extent, :] = total
        if chunk < chunks:
            own = pl.ds(level * share, share)
            ready[chunk, own] = ready[chunk, own] - obs[:, chunk * ROWS : (chunk + 1) * ROWS, :]
        for turn in range(1, depth):
            sum_copy(chunk, turn).start()

        @pl.when(jnp.logical_not(solver))
        def _():
            sum_copy(chunk, 0).start()

        if chunk < chunks:
            @pl.when(solver)
            def _():
                landed[tm, chunk, level] = ready[chunk, pl.ds(level * share, share)]

    def prepare():
        inverse_load.wait()
        square[:sensors, :sensors] = inverse_in[...]
        whole = square[...]
        high, low = split(whole)
        left_high[...] = high
        left_low[...] = low
        high, low = split(jnp.transpose(whole))
        inverse_cat[:, :width] = high
        inverse_cat[:, width:] = low
        coupling_load.wait()

    def compose(lag):
        square[:sensors, :sensors] = coupling_in[lag]
        high, low = split(square[...])
        for begin in range(0, width, TILE):
            end = min(begin + TILE, width)
            count = end - begin
            above = left_high[begin:end, :end]
            both = jnp.dot(
                jnp.concatenate([above, left_low[begin:end, :end]], axis=0), high[:end],
                preferred_element_type=F32,
            )
            rows = both[:count] + both[count:] + jnp.dot(above, low[:end], preferred_element_type=F32)
            turned = split(jnp.transpose(rows))
            place = pl.ds(pl.multiple_of(lag * width, LANES), width)
            weights[place, begin:end] = turned[0]
            weights[place, width + begin : width + end] = turned[1]

    map_load.wait()
    observed_load.wait()
    obs[...] = observed_in[pl.ds(core * half + side * group + level * share, share)].astype(F32)

    count = len(extents)
    soon, later = jnp.where(solver, 1, 0), jnp.where(solver, 3, 1)

    def when(step, act):
        for chunk in range(count):
            reached = step == chunk

            @pl.when(reached if chunk < chunks else reached & jnp.logical_not(solver))
            def _():
                act(chunk)

    def slot(index, carry):
        when(index, forward)

        @pl.when(solver & (index == chunks))
        def _():
            prepare()

        @pl.when(solver & (index >= chunks) & (index < chunks + band))
        def _():
            compose(index - chunks)

        when(index - soon, to_side)
        when(index - later, to_owner)
        return carry

    lax.fori_loop(0, jnp.where(solver, chunks + max(band, 3), count + 1), slot, 0)

    mine = pl.ds(core * half + side * group + level * share, share)
    last = planes * chunks * pieces - 1

    def out_copy(piece, turn, plane):
        local = piece - plane * chunks * pieces
        return remote(
            solved.at[piece], out_ref.at[mine, local],
            out_send.at[piece, turn], out_recv.at[local, level], along(turn, plane),
        )

    def last_copy(turn, other):
        return remote(
            solved.at[last], out_ref.at[mine, chunks * pieces - 1],
            last_send.at[turn, other - 1], last_recv.at[other - 1, level], along(turn, planes - 1, other),
        )

    def straight(piece):
        return solver & (piece == chunks * pieces - 1)

    def over_copy(piece, turn):
        block = out_ref.at[pl.ds(core * half + side * group, group), piece]
        return remote(
            block, block, over_send.at[piece, turn - 1], over_recv.at[piece, turn - 1], beside(turn)
        )

    def hand_over(piece):
        def block(turn, distance):
            first = core * half + lax.rem(side + turn, breadth) * group + lax.rem(level + distance, depth) * share
            return out_ref.at[pl.ds(first, share), piece]

        def arrival(source, semaphore):
            remote(source, source, mate_send.at[0], semaphore, mate).wait_recv()

        for distance in range(depth):
            source = block(0, distance)
            semaphore = out_recv.at[piece, lax.rem(level + distance, depth)]
            if distance:
                arrival(source, semaphore)
            else:
                @pl.when(jnp.logical_not(solver))
                def _():
                    arrival(source, semaphore)

        @pl.when(straight(piece))
        def _():
            for turn in range(1, breadth):
                for distance in range(depth):
                    semaphore = last_recv.at[breadth - turn - 1, lax.rem(level + distance, depth)]
                    arrival(block(turn, distance), semaphore)

        @pl.when(jnp.logical_not(straight(piece)))
        def _():
            for turn in range(1, breadth):
                over_copy(piece, turn).start()

    row = lax.broadcasted_iota(jnp.int32, (ROWS, width), 0)
    inner = lax.rem(row, SPAN)

    def advance(chunk, past):
        one, two, three = past
        plane = lax.div(chunk, chunks)
        local = lax.rem(chunk, chunks)

        def collect(buffer, semaphores, expected, origin):
            total = None
            for turn in range(depth):
                source = lax.rem(level + turn, depth)
                place = buffer.at[plane, local, source, :, pl.ds(0, expected)]
                arrival = remote(place, place, sum_send.at[0, 0], semaphores.at[plane, local, source], mate)
                if turn:
                    arrival.wait_recv()
                else:
                    @pl.when(origin != planes - 1)
                    def _():
                        arrival.wait_recv()
                term = buffer[plane, local, source]
                total = term if total is None else total + term
            return total

        misfit[:, :, :sensors] = -collect(landed, sum_recv, ROWS, plane)
        for spill, extent in enumerate(spill_extents()):
            @pl.when((plane > 0) & (local == spill))
            def _():
                more = collect(spilled, spill_recv, extent, plane - 1)
                misfit[:, :, :sensors] = misfit[:, :, :sensors] - more

        base = product(misfit[...].reshape(share * ROWS, width), inverse_cat[...])
        for block in range(ROWS // PACE):
            now = jnp.zeros((ROWS, width), F32)
            for sample in range(share):
                rows = base[sample * ROWS : (sample + 1) * ROWS]
                shift = (sample * SPAN - PACE * block) % ROWS
                rows = pltpu.roll(rows, shift, 0) if shift else rows
                begin = sample * SPAN
                now = jnp.where((row >= begin) & (row < begin + PACE), rows, now)
            carry = product(jnp.concatenate([one, two, three], axis=-1), weights[...])
            now = now - carry
            down = jnp.where(inner == 1, pltpu.roll(now, 1, 0), 0.0)
            now = now - product(down, weights[:width, :])
            piece = chunk * pieces + (block * PACE) // PIECE
            begin = (block * PACE) % PIECE
            for sample in range(share):
                rows = now[sample * SPAN : sample * SPAN + PACE, :sensors]
                solved[piece, sample, begin : begin + PACE, :] = rows
            one = jnp.where(inner == 0, pltpu.roll(now, ROWS - 1, 0), 0.0)
            three = jnp.where(inner == 0, pltpu.roll(two, ROWS - 1, 0), down)
            three = jnp.where(inner == 1, pltpu.roll(now, 1, 0), three)
            two = now
            if begin + PACE == PIECE:
                for turn in range(depth):
                    if turn:
                        out_copy(piece, turn, plane).start()
                    else:
                        @pl.when(plane != planes - 1)
                        def _():
                            out_copy(piece, 0, plane).start()

                        @pl.when(plane == planes - 1)
                        def _():
                            out_ref[mine, piece - plane * chunks * pieces] = solved[piece]

                @pl.when(piece == last)
                def _():
                    for turn in range(depth):
                        for other in range(1, breadth):
                            last_copy(turn, other).start()

                older = piece - LAG - tm * chunks * pieces

                @pl.when((older >= 0) & (older < chunks * pieces))
                def _():
                    hand_over(older)
        return one, two, three

    @pl.when(solver)
    def _():
        nothing = jnp.zeros((ROWS, width), F32)
        lax.fori_loop(0, planes * chunks, advance, (nothing,) * 3)

    def mate_copy(piece):
        block = out_ref.at[pl.ds(core * half, half), piece]
        return remote(block, block, mate_send.at[piece], mate_recv.at[piece], mate)

    done = jnp.where(solver, max(chunks * pieces - LAG, 0), 0)

    def finish(step, carry):
        @pl.when((step >= done) & (step < chunks * pieces))
        def _():
            hand_over(step)

        @pl.when(step > 0)
        def _():
            piece = step - 1

            @pl.when(jnp.logical_not(straight(piece)))
            def _():
                for turn in range(1, breadth):
                    over_copy(piece, turn).wait_recv()

            mate_copy(piece).start()

        return carry

    lax.fori_loop(0, chunks * pieces + 1, finish, 0)

    def settle(piece, carry):
        plane = lax.div(piece, chunks * pieces)
        for turn in range(depth):
            if turn:
                out_copy(piece, turn, plane).wait_send()
            else:
                @pl.when(plane != planes - 1)
                def _():
                    out_copy(piece, 0, plane).wait_send()
        return carry

    @pl.when(solver)
    def _():
        lax.fori_loop(0, planes * chunks * pieces, settle, 0)
        for turn in range(depth):
            for other in range(1, breadth):
                last_copy(turn, other).wait_send()

    def release(chunk):
        pair_copy(chunk).wait_send()
        for turn in range(1, breadth):
            side_copy(chunk, turn).wait_send()
        for turn in range(1, depth):
            sum_copy(chunk, turn).wait_send()

        @pl.when(jnp.logical_not(solver))
        def _():
            sum_copy(chunk, 0).wait_send()

    for chunk in range(count):
        if chunk < chunks:
            release(chunk)
        else:
            @pl.when(tm < planes - 1)
            def _():
                release(chunk)
    for piece in range(chunks * pieces):
        @pl.when(jnp.logical_not(straight(piece)))
        def _():
            for turn in range(1, breadth):
                over_copy(piece, turn).wait_send()

        mate_copy(piece).wait_send()
        mate_copy(piece).wait_recv()


def per_device(params, kernel, lag_offsets, observed, diag_inverse, coupling):
    samples, steps, cols = params.shape
    lags, _, sensors = kernel.shape
    band = coupling.shape[0]
    width = -(-sensors // LANES) * LANES
    depth, breadth = layout()
    planes = lax.axis_size("tm")
    chunks = steps // ROWS
    share = samples // (2 * depth * breadth)
    group = depth * share
    half = samples // 2
    pieces = ROWS // PIECE
    spills = len(spill_extents())
    vmem, dma = pltpu.VMEM, pltpu.SemaphoreType.DMA
    hbm = pl.BlockSpec(memory_space=pl.ANY)
    gathered = pl.pallas_call(
        whole_kernel,
        out_shape=jax.ShapeDtypeStruct((samples, steps // PIECE, PIECE, sensors), F32),
        in_specs=[hbm, hbm, pl.BlockSpec(memory_space=pltpu.SMEM), hbm, hbm, hbm],
        out_specs=pl.BlockSpec(memory_space=pltpu.VMEM),
        scratch_shapes=[
            vmem(params.shape, BF16),
            vmem((lags, sensors, cols), BF16),
            vmem(observed.shape, BF16),
            vmem(diag_inverse.shape, F32),
            vmem(coupling.shape, F32),
            vmem((REACH - 1 + (chunks + spills) * ROWS, samples, cols), BF16),
            vmem((chunks + spills, samples, ROWS, sensors), F32),
            vmem((chunks + spills, half, ROWS, sensors), F32),
            vmem((chunks + spills, half, ROWS, sensors), F32),
            vmem((chunks + spills, breadth - 1, group, ROWS, sensors), F32),
            vmem((chunks + spills, group, ROWS, sensors), F32),
            vmem((planes, chunks, depth, share, ROWS, sensors), F32),
            vmem((planes, spills, depth, share, ROWS, sensors), F32),
            vmem((share, steps, sensors), F32),
            vmem((width, width), F32),
            vmem((width, width), BF16),
            vmem((width, width), BF16),
            vmem((width, 2 * width), BF16),
            vmem((band * width, 2 * width), BF16),
            vmem((share, ROWS, width), F32),
            vmem((planes * chunks * pieces, share, PIECE, sensors), F32),
            dma((5,)),
            dma((chunks + spills,)),
            dma((chunks + spills,)),
            dma((chunks + spills, breadth - 1)),
            dma((chunks + spills, breadth - 1)),
            dma((chunks + spills, depth)),
            dma((planes, chunks, depth)),
            dma((planes, spills, depth)),
            dma((planes * chunks * pieces, depth)),
            dma((chunks * pieces, depth)),
            dma((depth, breadth - 1)),
            dma((breadth - 1, depth)),
            dma((chunks * pieces, breadth - 1)),
            dma((chunks * pieces, breadth - 1)),
            dma((chunks * pieces,)),
            dma((chunks * pieces,)),
        ],
        compiler_params=pltpu.CompilerParams(
            collective_id=0, has_side_effects=True, vmem_limit_bytes=60 * 2**20
        ),
    )(params, jnp.swapaxes(kernel, 1, 2), lag_offsets, observed, diag_inverse, coupling)
    return gathered.reshape(samples, steps, sensors)


def solution(mesh):
    in_specs = (P(None, "tm", "param"), P(None, "param", None), P(), P(None, "tm", None), P(), P())
    out_specs = P(None, "tm", None)
    return jax.shard_map(
        per_device, mesh=mesh, in_specs=in_specs, out_specs=out_specs, check_vma=False
    )
```

```python
import math
import jax
import jax.numpy as jnp
from jax import lax
from jax.experimental import pallas as pl
from jax.experimental.pallas import tpu as pltpu
from jax.sharding import PartitionSpec as P

REACH = 12
LANES = 128
TILE = 256
ROWS = 8
PIECE = 4
PACES = (2, 3, 3)
SPAN = 4
LAG = 2
LEVELS = 4
MESH = pl.DeviceIdType.MESH
F32 = jnp.float32
BF16 = jnp.bfloat16
ACROSS = (((1,), (1,)), ((), ()))


def split(value):
    high = value.astype(BF16)
    return high, (value - high.astype(F32)).astype(BF16)


def stack(value):
    return jnp.concatenate(split(value), axis=0)


def product(left, right):
    rows, width = left.shape[0], right.shape[1] // 2
    both = jnp.dot(stack(left), right, preferred_element_type=F32)
    return both[:rows, :width] + both[rows:, :width] + both[:rows, width:]


def layout():
    chips = lax.axis_size("param") // 2
    depth = math.gcd(chips, LEVELS)
    return depth, chips // depth


def spill_extents():
    rim = REACH - 1
    return tuple(-(-min(rim - begin, ROWS) // PIECE) * PIECE for begin in range(0, rim, ROWS))


def whole_kernel(
    params_ref, map_ref, lag_ref, observed_ref, inverse_ref, coupling_ref, out_ref,
    params_in, map_in, observed_in, inverse_in, coupling_in,
    window, part, pair_in, partial, side_in, ready, landed, spilled, obs, square, left_high, left_low,
    inverse_cat, weights, misfit, solved,
    load_sem, pair_send, pair_recv, side_send, side_recv, sum_send, sum_recv, spill_recv,
    out_send, out_recv, last_send, last_recv, over_send, over_recv, mate_send, mate_recv,
):
    samples, steps, cols = params_ref.shape
    lags, sensors, _ = map_ref.shape
    band = coupling_ref.shape[0]
    width = square.shape[0]
    chunks = steps // ROWS
    rim = REACH - 1
    spills = -(-rim // ROWS)
    extents = (ROWS,) * chunks + spill_extents()
    me, tm = lax.axis_index("param"), lax.axis_index("tm")
    depth, breadth = layout()
    core, side, level = lax.rem(me, 2), lax.rem(lax.div(me, 2), breadth), lax.div(me, 2 * breadth)
    planes = lax.axis_size("tm")
    share = samples // (2 * depth * breadth)
    group = depth * share
    solver = tm == planes - 1
    half = samples // 2
    pieces = ROWS // PIECE

    def along(distance, plane, turn=0):
        other = lax.rem(level + distance, depth) * breadth + lax.rem(side + turn, breadth)
        return {"param": other * 2 + core, "tm": plane}

    def beside(distance):
        return {"param": (level * breadth + lax.rem(side + distance, breadth)) * 2 + core, "tm": tm}

    mate = {"param": me + 1 - 2 * core, "tm": tm}

    def remote(source, target, send_sem, recv_sem, device):
        return pltpu.make_async_remote_copy(
            src_ref=source, dst_ref=target, send_sem=send_sem, recv_sem=recv_sem,
            device_id=device, device_id_type=MESH,
        )

    barrier = pltpu.get_barrier_semaphore()
    loads = [
        pltpu.make_async_copy(source, target, load_sem.at[i])
        for i, (source, target) in enumerate((
            (params_ref, params_in), (map_ref, map_in), (observed_ref, observed_in),
            (inverse_ref, inverse_in), (coupling_ref, coupling_in),
        ))
    ]
    params_load, map_load, observed_load, inverse_load, coupling_load = loads
    for load in loads[:3]:
        load.start()

    @pl.when(solver)
    def _():
        inverse_load.start()
        coupling_load.start()

    pl.semaphore_signal(barrier, inc=1, device_id=mate, device_id_type=MESH)
    for turn in range(breadth):
        for distance in range(depth):
            for hop in range(planes):
                if turn or distance or hop:
                    device = along(distance, lax.rem(tm + hop, planes), turn)
                    pl.semaphore_signal(barrier, inc=1, device_id=device, device_id_type=MESH)

    misfit[...] = jnp.zeros_like(misfit)
    square[...] = jnp.zeros_like(square)

    params_load.wait()
    turned = jnp.swapaxes(params_in[...].astype(F32), 0, 1).astype(BF16)
    window[:rim] = jnp.zeros((rim, samples, cols), BF16)
    window[rim : rim + steps] = turned
    behind = window.shape[0] - rim - steps
    window[rim + steps :] = jnp.zeros((behind, samples, cols), BF16)
    for chunk, extent in enumerate(spill_extents()):
        if extent < ROWS:
            blank = jnp.zeros((planes, depth, share, ROWS - extent, sensors), F32)
            spilled[:, chunk, :, :, extent:, :] = blank
    pl.semaphore_wait(barrier, planes * depth * breadth)

    def pair_copy(chunk):
        return remote(
            part.at[chunk, pl.ds((1 - core) * half, half), pl.ds(0, extents[chunk])],
            pair_in.at[chunk, :, pl.ds(0, extents[chunk])],
            pair_send.at[chunk], pair_recv.at[chunk], mate,
        )

    def forward(chunk):
        extent = extents[chunk]
        total = None
        for lag in range(lags):
            start = rim + ROWS * chunk - lag_ref[lag]
            left = window[pl.ds(start, extent)].reshape(extent * samples, cols)
            term = lax.dot_general(left, map_in[lag], ACROSS, preferred_element_type=F32)
            total = term if total is None else total + term
        part[chunk, :, :extent, :] = jnp.swapaxes(total.reshape(extent, samples, sensors), 0, 1)
        pair_copy(chunk).start()

    def side_copy(chunk, turn):
        rows = pl.ds(0, extents[chunk])
        other = lax.rem(side + turn, breadth)
        return remote(
            partial.at[chunk, pl.ds(other * group, group), rows], side_in.at[chunk, turn - 1, :, rows],
            side_send.at[chunk, turn - 1], side_recv.at[chunk, turn - 1], beside(turn),
        )

    def to_side(chunk):
        extent = extents[chunk]
        pair_copy(chunk).wait_recv()
        partial[chunk, :, :extent, :] = (
            part[chunk, pl.ds(core * half, half), :extent, :] + pair_in[chunk, :, :extent, :]
        )
        for turn in range(1, breadth):
            side_copy(chunk, turn).start()

    def sum_copy(chunk, turn):
        rows = pl.ds(0, extents[chunk])
        if chunk < chunks:
            target, arrived = landed.at[tm, chunk, level], sum_recv.at[tm, chunk, level]
        else:
            target = spilled.at[tm + 1, chunk - chunks, level, :, rows]
            arrived = spill_recv.at[tm + 1, chunk - chunks, level]
        return remote(
            ready.at[chunk, pl.ds(lax.rem(level + turn, depth) * share, share), rows], target,
            sum_send.at[chunk, turn], arrived, along(turn, planes - 1),
        )

    def to_owner(chunk):
        extent = extents[chunk]
        total = partial[chunk, pl.ds(side * group, group), :extent, :]
        for turn in range(1, breadth):
            side_copy(chunk, turn).wait_recv()
            total = total + side_in[chunk, turn - 1, :, :extent, :]
        ready[chunk, :, :extent, :] = total
        if chunk < chunks:
            own = pl.ds(level * share, share)
            ready[chunk, own] = ready[chunk, own] - obs[:, chunk * ROWS : (chunk + 1) * ROWS, :]
        for turn in range(1, depth):
            sum_copy(chunk, turn).start()

        @pl.when(jnp.logical_not(solver))
        def _():
            sum_copy(chunk, 0).start()

        if chunk < chunks:
            @pl.when(solver)
            def _():
                landed[tm, chunk, level] = ready[chunk, pl.ds(level * share, share)]

    def prepare():
        inverse_load.wait()
        square[:sensors, :sensors] = inverse_in[...]
        whole = square[...]
        high, low = split(whole)
        left_high[...] = high
        left_low[...] = low
        high, low = split(jnp.transpose(whole))
        inverse_cat[:, :width] = high
        inverse_cat[:, width:] = low
        coupling_load.wait()

    def compose(lag):
        square[:sensors, :sensors] = coupling_in[lag]
        high, low = split(square[...])
        for begin in range(0, width, TILE):
            end = min(begin + TILE, width)
            count = end - begin
            above = left_high[begin:end, :end]
            both = jnp.dot(
                jnp.concatenate([above, left_low[begin:end, :end]], axis=0), high[:end],
                preferred_element_type=F32,
            )
            rows = both[:count] + both[count:] + jnp.dot(above, low[:end], preferred_element_type=F32)
            turned = split(jnp.transpose(rows))
            place = pl.ds(pl.multiple_of((lag + 1) * width, LANES), width)
            weights[place, begin:end] = turned[0]
            weights[place, width + begin : width + end] = turned[1]

    def extend():
        for begin in range(0, width, TILE):
            end = min(begin + TILE, width)
            count = end - begin
            above = weights[width + begin : width + end, :]
            both = jnp.dot(
                jnp.concatenate([above[:, :width], above[:, width:]], axis=0),
                weights[width : 2 * width, :width], preferred_element_type=F32,
            )
            rows = both[:count] + both[count:] + jnp.dot(
                above[:, :width], weights[width : 2 * width, width:], preferred_element_type=F32
            )
            direct = weights[2 * width + begin : 2 * width + end, :].astype(F32)
            high, low = split(direct[:, :width] + direct[:, width:] - rows)
            weights[begin:end, :width] = high
            weights[begin:end, width:] = low

    map_load.wait()
    observed_load.wait()
    obs[...] = observed_in[pl.ds(core * half + side * group + level * share, share)].astype(F32)

    count = len(extents)

    def when(step, act, delays=lambda chunk: (0, 0)):
        for chunk in range(count):
            reached = step == chunk + jnp.where(solver, *delays(chunk))

            @pl.when(reached if chunk < chunks else reached & jnp.logical_not(solver))
            def _():
                act(chunk)

    def slot(index, carry):
        when(index, forward)

        @pl.when(solver & (index == chunks))
        def _():
            prepare()

        @pl.when(solver & (index >= chunks) & (index < chunks + band))
        def _():
            compose(index - chunks)

        when(index, to_side, lambda chunk: (1, min(chunk, 1)))
        when(index, to_owner, lambda chunk: (3, 2 + min(chunk, 1)))

        @pl.when(solver & (index == chunks + band))
        def _():
            extend()

        return carry

    lax.fori_loop(0, jnp.where(solver, chunks + max(band, 3) + 1, count + 3), slot, 0)

    mine = pl.ds(core * half + side * group + level * share, share)
    last = planes * chunks * pieces - 1

    def out_copy(piece, turn, plane):
        local = piece - plane * chunks * pieces
        return remote(
            solved.at[piece], out_ref.at[mine, local],
            out_send.at[piece, turn], out_recv.at[local, level], along(turn, plane),
        )

    def last_copy(turn, other):
        return remote(
            solved.at[last], out_ref.at[mine, chunks * pieces - 1],
            last_send.at[turn, other - 1], last_recv.at[other - 1, level], along(turn, planes - 1, other),
        )

    def straight(piece):
        return solver & (piece == chunks * pieces - 1)

    def over_copy(piece, turn):
        block = out_ref.at[pl.ds(core * half + side * group, group), piece]
        return remote(
            block, block, over_send.at[piece, turn - 1], over_recv.at[piece, turn - 1], beside(turn)
        )

    def hand_over(piece):
        def block(turn, distance):
            first = core * half + lax.rem(side + turn, breadth) * group + lax.rem(level + distance, depth) * share
            return out_ref.at[pl.ds(first, share), piece]

        def arrival(source, semaphore):
            remote(source, source, mate_send.at[0], semaphore, mate).wait_recv()

        for distance in range(depth):
            source = block(0, distance)
            semaphore = out_recv.at[piece, lax.rem(level + distance, depth)]
            if distance:
                arrival(source, semaphore)
            else:
                @pl.when(jnp.logical_not(solver))
                def _():
                    arrival(source, semaphore)

        @pl.when(straight(piece))
        def _():
            for turn in range(1, breadth):
                for distance in range(depth):
                    semaphore = last_recv.at[breadth - turn - 1, lax.rem(level + distance, depth)]
                    arrival(block(turn, distance), semaphore)

        @pl.when(jnp.logical_not(straight(piece)))
        def _():
            for turn in range(1, breadth):
                over_copy(piece, turn).start()

    row = lax.broadcasted_iota(jnp.int32, (ROWS, width), 0)
    inner = lax.rem(row, SPAN)

    def advance(chunk, past):
        one, two, three = past
        plane = lax.div(chunk, chunks)
        local = lax.rem(chunk, chunks)

        def collect(buffer, semaphores, expected, origin):
            total = None
            for turn in range(depth):
                source = lax.rem(level + turn, depth)
                place = buffer.at[plane, local, source, :, pl.ds(0, expected)]
                arrival = remote(place, place, sum_send.at[0, 0], semaphores.at[plane, local, source], mate)
                if turn:
                    arrival.wait_recv()
                else:
                    @pl.when(origin != planes - 1)
                    def _():
                        arrival.wait_recv()
                term = buffer[plane, local, source]
                total = term if total is None else total + term
            return total

        misfit[:, :, :sensors] = -collect(landed, sum_recv, ROWS, plane)
        for spill, extent in enumerate(spill_extents()):
            @pl.when((plane > 0) & (local == spill))
            def _():
                more = collect(spilled, spill_recv, extent, plane - 1)
                misfit[:, :, :sensors] = misfit[:, :, :sensors] - more

        base = product(misfit[...].reshape(share * ROWS, width), inverse_cat[...])
        start = 0
        for pace in PACES:
            now = jnp.zeros((ROWS, width), F32)
            for sample in range(share):
                rows = base[sample * ROWS : (sample + 1) * ROWS]
                shift = (sample * SPAN - start) % ROWS
                rows = pltpu.roll(rows, shift, 0) if shift else rows
                begin = sample * SPAN
                now = jnp.where((row >= begin) & (row < begin + pace), rows, now)
            carry = product(jnp.concatenate([one, two, three], axis=-1), weights[width:, :])
            now = jnp.where(inner < pace, now - carry, 0.0)
            down = jnp.where((inner > 0) & (inner < pace), pltpu.roll(now, 1, 0), 0.0)
            if pace == 2:
                now = now - product(down, weights[width : 2 * width, :])
                three = jnp.where(inner == 0, pltpu.roll(three, ROWS - 2, 0), 0.0)
                three = jnp.where((inner == 1) | (inner == 2), pltpu.roll(now, 1, 0), three)
                two = now
            else:
                far = jnp.where(inner == 2, pltpu.roll(now, 2, 0), 0.0)
                now = now - product(jnp.concatenate([far, down], axis=-1), weights[: 2 * width, :])
                three = now
                two = jnp.where(inner < 2, pltpu.roll(now, ROWS - 1, 0), 0.0)
            one = jnp.where(inner == 0, pltpu.roll(now, ROWS - (pace - 1), 0), 0.0)
            for part_of in range(pieces):
                begin = max(start, part_of * PIECE)
                end = min(start + pace, (part_of + 1) * PIECE)
                for sample in range(share):
                    if begin < end:
                        place = sample * SPAN - start
                        rows = now[place + begin : place + end, :sensors]
                        target = pl.ds(begin - part_of * PIECE, end - begin)
                        solved[chunk * pieces + part_of, sample, target, :] = rows
            full = (start + pace) // PIECE
            piece = chunk * pieces + full - 1
            fresh = full > start // PIECE
            start += pace
            if fresh:
                for turn in range(depth):
                    if turn:
                        out_copy(piece, turn, plane).start()
                    else:
                        @pl.when(plane != planes - 1)
                        def _():
                            out_copy(piece, 0, plane).start()

                        @pl.when(plane == planes - 1)
                        def _():
                            out_ref[mine, piece - plane * chunks * pieces] = solved[piece]

                @pl.when(piece == last)
                def _():
                    for turn in range(depth):
                        for other in range(1, breadth):
                            last_copy(turn, other).start()

                older = piece - LAG - tm * chunks * pieces

                @pl.when((older >= 0) & (older < chunks * pieces))
                def _():
                    hand_over(older)
        return one, two, three

    @pl.when(solver)
    def _():
        nothing = jnp.zeros((ROWS, width), F32)
        lax.fori_loop(0, planes * chunks, advance, (nothing,) * 3)

    def mate_copy(piece):
        block = out_ref.at[pl.ds(core * half, half), piece]
        return remote(block, block, mate_send.at[piece], mate_recv.at[piece], mate)

    done = jnp.where(solver, max(chunks * pieces - LAG, 0), 0)

    def finish(step, carry):
        @pl.when((step >= done) & (step < chunks * pieces))
        def _():
            hand_over(step)

        @pl.when(step > 0)
        def _():
            piece = step - 1

            @pl.when(jnp.logical_not(straight(piece)))
            def _():
                for turn in range(1, breadth):
                    over_copy(piece, turn).wait_recv()

            mate_copy(piece).start()

        return carry

    lax.fori_loop(0, chunks * pieces + 1, finish, 0)

    def settle(piece, carry):
        plane = lax.div(piece, chunks * pieces)
        for turn in range(depth):
            if turn:
                out_copy(piece, turn, plane).wait_send()
            else:
                @pl.when(plane != planes - 1)
                def _():
                    out_copy(piece, 0, plane).wait_send()
        return carry

    @pl.when(solver)
    def _():
        lax.fori_loop(0, planes * chunks * pieces, settle, 0)
        for turn in range(depth):
            for other in range(1, breadth):
                last_copy(turn, other).wait_send()

    def release(chunk):
        pair_copy(chunk).wait_send()
        for turn in range(1, breadth):
            side_copy(chunk, turn).wait_send()
        for turn in range(1, depth):
            sum_copy(chunk, turn).wait_send()

        @pl.when(jnp.logical_not(solver))
        def _():
            sum_copy(chunk, 0).wait_send()

    for chunk in range(count):
        if chunk < chunks:
            release(chunk)
        else:
            @pl.when(tm < planes - 1)
            def _():
                release(chunk)
    for piece in range(chunks * pieces):
        @pl.when(jnp.logical_not(straight(piece)))
        def _():
            for turn in range(1, breadth):
                over_copy(piece, turn).wait_send()

        mate_copy(piece).wait_send()
        mate_copy(piece).wait_recv()


def per_device(params, kernel, lag_offsets, observed, diag_inverse, coupling):
    samples, steps, cols = params.shape
    lags, _, sensors = kernel.shape
    band = coupling.shape[0]
    width = -(-sensors // LANES) * LANES
    depth, breadth = layout()
    planes = lax.axis_size("tm")
    chunks = steps // ROWS
    share = samples // (2 * depth * breadth)
    group = depth * share
    half = samples // 2
    pieces = ROWS // PIECE
    spills = len(spill_extents())
    vmem, dma = pltpu.VMEM, pltpu.SemaphoreType.DMA
    hbm = pl.BlockSpec(memory_space=pl.ANY)
    gathered = pl.pallas_call(
        whole_kernel,
        out_shape=jax.ShapeDtypeStruct((samples, steps // PIECE, PIECE, sensors), F32),
        in_specs=[hbm, hbm, pl.BlockSpec(memory_space=pltpu.SMEM), hbm, hbm, hbm],
        out_specs=pl.BlockSpec(memory_space=pltpu.VMEM),
        scratch_shapes=[
            vmem(params.shape, BF16),
            vmem((lags, sensors, cols), BF16),
            vmem(observed.shape, BF16),
            vmem(diag_inverse.shape, F32),
            vmem(coupling.shape, F32),
            vmem((REACH - 1 + (chunks + spills) * ROWS, samples, cols), BF16),
            vmem((chunks + spills, samples, ROWS, sensors), F32),
            vmem((chunks + spills, half, ROWS, sensors), F32),
            vmem((chunks + spills, half, ROWS, sensors), F32),
            vmem((chunks + spills, breadth - 1, group, ROWS, sensors), F32),
            vmem((chunks + spills, group, ROWS, sensors), F32),
            vmem((planes, chunks, depth, share, ROWS, sensors), F32),
            vmem((planes, spills, depth, share, ROWS, sensors), F32),
            vmem((share, steps, sensors), F32),
            vmem((width, width), F32),
            vmem((width, width), BF16),
            vmem((width, width), BF16),
            vmem((width, 2 * width), BF16),
            vmem(((band + 1) * width, 2 * width), BF16),
            vmem((share, ROWS, width), F32),
            vmem((planes * chunks * pieces, share, PIECE, sensors), F32),
            dma((5,)),
            dma((chunks + spills,)),
            dma((chunks + spills,)),
            dma((chunks + spills, breadth - 1)),
            dma((chunks + spills, breadth - 1)),
            dma((chunks + spills, depth)),
            dma((planes, chunks, depth)),
            dma((planes, spills, depth)),
            dma((planes * chunks * pieces, depth)),
            dma((chunks * pieces, depth)),
            dma((depth, breadth - 1)),
            dma((breadth - 1, depth)),
            dma((chunks * pieces, breadth - 1)),
            dma((chunks * pieces, breadth - 1)),
            dma((chunks * pieces,)),
            dma((chunks * pieces,)),
        ],
        compiler_params=pltpu.CompilerParams(
            collective_id=0, has_side_effects=True, vmem_limit_bytes=60 * 2**20
        ),
    )(params, jnp.swapaxes(kernel, 1, 2), lag_offsets, observed, diag_inverse, coupling)
    return gathered.reshape(samples, steps, sensors)


def solution(mesh):
    in_specs = (P(None, "tm", "param"), P(None, "param", None), P(), P(None, "tm", None), P(), P())
    out_specs = P(None, "tm", None)
    return jax.shard_map(
        per_device, mesh=mesh, in_specs=in_specs, out_specs=out_specs, check_vma=False
    )
```

```python
import math
import jax
import jax.numpy as jnp
from jax import lax
from jax.experimental import pallas as pl
from jax.experimental.pallas import tpu as pltpu
from jax.sharding import PartitionSpec as P

REACH = 12
LANES = 128
TILE = 256
ROWS = 8
PIECE = 4
PACES = (2, 3, 3)
SPAN = 4
LAG = 2
LEVELS = 4
MESH = pl.DeviceIdType.MESH
F32 = jnp.float32
BF16 = jnp.bfloat16
ACROSS = (((1,), (1,)), ((), ()))


def split(value):
    high = value.astype(BF16)
    return high, (value - high.astype(F32)).astype(BF16)


def stack(value):
    return jnp.concatenate(split(value), axis=0)


def product(left, right):
    rows, width = left.shape[0], right.shape[1] // 2
    both = jnp.dot(stack(left), right, preferred_element_type=F32)
    return both[:rows, :width] + both[rows:, :width] + both[:rows, width:]


def layout():
    chips = lax.axis_size("param") // 2
    depth = math.gcd(chips, LEVELS)
    return depth, chips // depth


def spill_extents():
    rim = REACH - 1
    return tuple(-(-min(rim - begin, ROWS) // PIECE) * PIECE for begin in range(0, rim, ROWS))


def whole_kernel(
    params_ref, map_ref, lag_ref, observed_ref, inverse_ref, coupling_ref, out_ref,
    params_in, map_in, observed_in, inverse_in, coupling_in,
    window, part, pair_in, partial, side_in, ready, landed, spilled, obs, square, left_high, left_low,
    inverse_cat, weights, misfit, solved,
    load_sem, pair_send, pair_recv, side_send, side_recv, sum_send, sum_recv, spill_recv,
    out_send, out_recv, last_send, last_recv, over_send, over_recv, mate_send, mate_recv,
):
    samples, steps, cols = params_ref.shape
    lags, sensors, _ = map_ref.shape
    band = coupling_ref.shape[0]
    width = square.shape[0]
    chunks = steps // ROWS
    rim = REACH - 1
    spills = -(-rim // ROWS)
    extents = (ROWS,) * chunks + spill_extents()
    me, tm = lax.axis_index("param"), lax.axis_index("tm")
    depth, breadth = layout()
    core, side, level = lax.rem(me, 2), lax.rem(lax.div(me, 2), breadth), lax.div(me, 2 * breadth)
    planes = lax.axis_size("tm")
    share = samples // (2 * depth * breadth)
    group = depth * share
    solver = tm == planes - 1
    half = samples // 2
    pieces = ROWS // PIECE

    def along(distance, plane, turn=0):
        other = lax.rem(level + distance, depth) * breadth + lax.rem(side + turn, breadth)
        return {"param": other * 2 + core, "tm": plane}

    def beside(distance):
        return {"param": (level * breadth + lax.rem(side + distance, breadth)) * 2 + core, "tm": tm}

    mate = {"param": me + 1 - 2 * core, "tm": tm}

    def remote(source, target, send_sem, recv_sem, device):
        return pltpu.make_async_remote_copy(
            src_ref=source, dst_ref=target, send_sem=send_sem, recv_sem=recv_sem,
            device_id=device, device_id_type=MESH,
        )

    barrier = pltpu.get_barrier_semaphore()
    loads = [
        pltpu.make_async_copy(source, target, load_sem.at[i])
        for i, (source, target) in enumerate((
            (params_ref, params_in), (map_ref, map_in), (observed_ref, observed_in),
            (inverse_ref, inverse_in), (coupling_ref, coupling_in),
        ))
    ]
    params_load, map_load, observed_load, inverse_load, coupling_load = loads
    for load in loads[:3]:
        load.start()

    @pl.when(solver)
    def _():
        inverse_load.start()
        coupling_load.start()

    pl.semaphore_signal(barrier, inc=1, device_id=mate, device_id_type=MESH)
    for turn in range(breadth):
        for distance in range(depth):
            for hop in range(planes):
                if turn or distance or hop:
                    device = along(distance, lax.rem(tm + hop, planes), turn)
                    pl.semaphore_signal(barrier, inc=1, device_id=device, device_id_type=MESH)

    misfit[...] = jnp.zeros_like(misfit)
    square[...] = jnp.zeros_like(square)

    params_load.wait()
    turned = jnp.swapaxes(params_in[...].astype(F32), 0, 1).astype(BF16)
    window[:rim] = jnp.zeros((rim, samples, cols), BF16)
    window[rim : rim + steps] = turned
    behind = window.shape[0] - rim - steps
    window[rim + steps :] = jnp.zeros((behind, samples, cols), BF16)
    for chunk, extent in enumerate(spill_extents()):
        if extent < ROWS:
            blank = jnp.zeros((planes, depth, share, ROWS - extent, sensors), F32)
            spilled[:, chunk, :, :, extent:, :] = blank
    pl.semaphore_wait(barrier, planes * depth * breadth)

    def pair_copy(chunk):
        return remote(
            part.at[chunk, pl.ds((1 - core) * half, half), pl.ds(0, extents[chunk])],
            pair_in.at[chunk, :, pl.ds(0, extents[chunk])],
            pair_send.at[chunk], pair_recv.at[chunk], mate,
        )

    def forward(chunk):
        extent = extents[chunk]
        total = None
        for lag in range(lags):
            start = rim + ROWS * chunk - lag_ref[lag]
            left = window[pl.ds(start, extent)].reshape(extent * samples, cols)
            term = lax.dot_general(left, map_in[lag], ACROSS, preferred_element_type=F32)
            total = term if total is None else total + term
        part[chunk, :, :extent, :] = jnp.swapaxes(total.reshape(extent, samples, sensors), 0, 1)
        pair_copy(chunk).start()

    def side_copy(chunk, turn):
        rows = pl.ds(0, extents[chunk])
        other = lax.rem(side + turn, breadth)
        return remote(
            partial.at[chunk, pl.ds(other * group, group), rows], side_in.at[chunk, turn - 1, :, rows],
            side_send.at[chunk, turn - 1], side_recv.at[chunk, turn - 1], beside(turn),
        )

    def to_side(chunk):
        extent = extents[chunk]
        pair_copy(chunk).wait_recv()
        partial[chunk, :, :extent, :] = (
            part[chunk, pl.ds(core * half, half), :extent, :] + pair_in[chunk, :, :extent, :]
        )
        for turn in range(1, breadth):
            side_copy(chunk, turn).start()

    def sum_copy(chunk, turn):
        rows = pl.ds(0, extents[chunk])
        if chunk < chunks:
            target, arrived = landed.at[tm, chunk, level], sum_recv.at[tm, chunk, level]
        else:
            target = spilled.at[tm + 1, chunk - chunks, level, :, rows]
            arrived = spill_recv.at[tm + 1, chunk - chunks, level]
        return remote(
            ready.at[chunk, pl.ds(lax.rem(level + turn, depth) * share, share), rows], target,
            sum_send.at[chunk, turn], arrived, along(turn, planes - 1),
        )

    def to_owner(chunk):
        extent = extents[chunk]
        total = partial[chunk, pl.ds(side * group, group), :extent, :]
        for turn in range(1, breadth):
            side_copy(chunk, turn).wait_recv()
            total = total + side_in[chunk, turn - 1, :, :extent, :]
        ready[chunk, :, :extent, :] = total
        if chunk < chunks:
            own = pl.ds(level * share, share)
            ready[chunk, own] = ready[chunk, own] - obs[:, chunk * ROWS : (chunk + 1) * ROWS, :]
        for turn in range(1, depth):
            sum_copy(chunk, turn).start()

        @pl.when(jnp.logical_not(solver))
        def _():
            sum_copy(chunk, 0).start()

        if chunk < chunks:
            @pl.when(solver)
            def _():
                landed[tm, chunk, level] = ready[chunk, pl.ds(level * share, share)]

    def prepare():
        inverse_load.wait()
        square[:sensors, :sensors] = inverse_in[...]
        whole = square[...]
        high, low = split(whole)
        left_high[...] = high
        left_low[...] = low
        high, low = split(jnp.transpose(whole))
        inverse_cat[:, :width] = high
        inverse_cat[:, width:] = low
        coupling_load.wait()

    def compose(lag):
        square[:sensors, :sensors] = coupling_in[lag]
        high, low = split(square[...])
        for begin in range(0, width, TILE):
            end = min(begin + TILE, width)
            count = end - begin
            above = left_high[begin:end, :end]
            both = jnp.dot(
                jnp.concatenate([above, left_low[begin:end, :end]], axis=0), high[:end],
                preferred_element_type=F32,
            )
            rows = both[:count] + both[count:] + jnp.dot(above, low[:end], preferred_element_type=F32)
            turned = split(jnp.transpose(rows))
            place = pl.ds(pl.multiple_of((lag + 1) * width, LANES), width)
            weights[place, begin:end] = turned[0]
            weights[place, width + begin : width + end] = turned[1]

    def extend():
        for begin in range(0, width, TILE):
            end = min(begin + TILE, width)
            count = end - begin
            above = weights[width + begin : width + end, :]
            both = jnp.dot(
                jnp.concatenate([above[:, :width], above[:, width:]], axis=0),
                weights[width : 2 * width, :width], preferred_element_type=F32,
            )
            rows = both[:count] + both[count:] + jnp.dot(
                above[:, :width], weights[width : 2 * width, width:], preferred_element_type=F32
            )
            direct = weights[2 * width + begin : 2 * width + end, :].astype(F32)
            high, low = split(direct[:, :width] + direct[:, width:] - rows)
            weights[begin:end, :width] = high
            weights[begin:end, width:] = low

    map_load.wait()
    observed_load.wait()
    obs[...] = observed_in[pl.ds(core * half + side * group + level * share, share)].astype(F32)

    count = len(extents)

    def when(step, act, delays=lambda chunk: (0, 0)):
        for chunk in range(count):
            reached = step == chunk + jnp.where(solver, *delays(chunk))

            @pl.when(reached if chunk < chunks else reached & jnp.logical_not(solver))
            def _():
                act(chunk)

    def slot(index, carry):
        when(index, forward)

        @pl.when(solver & (index == chunks))
        def _():
            prepare()

        @pl.when(solver & (index >= chunks) & (index < chunks + band))
        def _():
            compose(index - chunks)

        when(index, to_side, lambda chunk: (1, min(chunk, 1)))
        when(index, to_owner, lambda chunk: (3, 2 + min(chunk, 1)))

        @pl.when(solver & (index == chunks + band))
        def _():
            extend()

        return carry

    lax.fori_loop(0, jnp.where(solver, chunks + max(band, 3) + 1, count + 3), slot, 0)

    mine = pl.ds(core * half + side * group + level * share, share)
    last = planes * chunks * pieces - 1

    def out_copy(piece, turn, plane):
        local = piece - plane * chunks * pieces
        return remote(
            solved.at[piece], out_ref.at[mine, local],
            out_send.at[piece, turn], out_recv.at[local, level], along(turn, plane),
        )

    def last_copy(turn, other):
        return remote(
            solved.at[last], out_ref.at[mine, chunks * pieces - 1],
            last_send.at[turn, other - 1], last_recv.at[other - 1, level], along(turn, planes - 1, other),
        )

    def straight(piece):
        return solver & (piece == chunks * pieces - 1)

    def over_copy(piece, turn):
        block = out_ref.at[pl.ds(core * half + side * group, group), piece]
        return remote(
            block, block, over_send.at[piece, turn - 1], over_recv.at[piece, turn - 1], beside(turn)
        )

    def hand_over(piece):
        def block(turn, distance):
            first = core * half + lax.rem(side + turn, breadth) * group + lax.rem(level + distance, depth) * share
            return out_ref.at[pl.ds(first, share), piece]

        def arrival(source, semaphore):
            remote(source, source, mate_send.at[0], semaphore, mate).wait_recv()

        for distance in range(depth):
            source = block(0, distance)
            semaphore = out_recv.at[piece, lax.rem(level + distance, depth)]
            if distance:
                arrival(source, semaphore)
            else:
                @pl.when(jnp.logical_not(solver))
                def _():
                    arrival(source, semaphore)

        @pl.when(straight(piece))
        def _():
            for turn in range(1, breadth):
                for distance in range(depth):
                    semaphore = last_recv.at[breadth - turn - 1, lax.rem(level + distance, depth)]
                    arrival(block(turn, distance), semaphore)

        @pl.when(jnp.logical_not(straight(piece)))
        def _():
            for turn in range(1, breadth):
                over_copy(piece, turn).start()

    row = lax.broadcasted_iota(jnp.int32, (ROWS, width), 0)
    inner = lax.rem(row, SPAN)

    def advance(chunk, past):
        one, two, three = past
        plane = lax.div(chunk, chunks)
        local = lax.rem(chunk, chunks)

        def collect(buffer, semaphores, expected, origin):
            total = None
            for turn in range(depth):
                source = lax.rem(level + turn, depth)
                place = buffer.at[plane, local, source, :, pl.ds(0, expected)]
                arrival = remote(place, place, sum_send.at[0, 0], semaphores.at[plane, local, source], mate)
                if turn:
                    arrival.wait_recv()
                else:
                    @pl.when(origin != planes - 1)
                    def _():
                        arrival.wait_recv()
                term = buffer[plane, local, source]
                total = term if total is None else total + term
            return total

        misfit[:, :, :sensors] = -collect(landed, sum_recv, ROWS, plane)
        for spill, extent in enumerate(spill_extents()):
            @pl.when((plane > 0) & (local == spill))
            def _():
                more = collect(spilled, spill_recv, extent, plane - 1)
                misfit[:, :, :sensors] = misfit[:, :, :sensors] - more

        base = product(misfit[...].reshape(share * ROWS, width), inverse_cat[...])
        start = 0
        for pace in PACES:
            now = jnp.zeros((ROWS, width), F32)
            for sample in range(share):
                rows = base[sample * ROWS : (sample + 1) * ROWS]
                shift = (sample * SPAN - start) % ROWS
                rows = pltpu.roll(rows, shift, 0) if shift else rows
                begin = sample * SPAN
                now = jnp.where((row >= begin) & (row < begin + pace), rows, now)
            carry = product(jnp.concatenate([one, two, three], axis=-1), weights[width:, :])
            now = jnp.where(inner < pace, now - carry, 0.0)
            down = jnp.where((inner > 0) & (inner < pace), pltpu.roll(now, 1, 0), 0.0)
            if pace == 2:
                now = now - product(down, weights[width : 2 * width, :])
                three = jnp.where(inner == 0, pltpu.roll(three, ROWS - 2, 0), 0.0)
                three = jnp.where((inner == 1) | (inner == 2), pltpu.roll(now, 1, 0), three)
                two = now
            else:
                far = jnp.where(inner == 2, pltpu.roll(now, 2, 0), 0.0)
                now = now - product(jnp.concatenate([far, down], axis=-1), weights[: 2 * width, :])
                three = now
                two = jnp.where(inner < 2, pltpu.roll(now, ROWS - 1, 0), 0.0)
            one = jnp.where(inner == 0, pltpu.roll(now, ROWS - (pace - 1), 0), 0.0)
            for part_of in range(pieces):
                begin = max(start, part_of * PIECE)
                end = min(start + pace, (part_of + 1) * PIECE)
                for sample in range(share):
                    if begin < end:
                        place = sample * SPAN - start
                        rows = now[place + begin : place + end, :sensors]
                        target = pl.ds(begin - part_of * PIECE, end - begin)
                        solved[chunk * pieces + part_of, sample, target, :] = rows
            full = (start + pace) // PIECE
            piece = chunk * pieces + full - 1
            fresh = full > start // PIECE
            start += pace
            if fresh:
                @pl.when(piece == last)
                def _():
                    for turn in range(depth):
                        for other in range(1, breadth):
                            last_copy(turn, other).start()

                for turn in range(depth):
                    if turn:
                        out_copy(piece, turn, plane).start()
                    else:
                        @pl.when(plane != planes - 1)
                        def _():
                            out_copy(piece, 0, plane).start()

                        @pl.when(plane == planes - 1)
                        def _():
                            out_ref[mine, piece - plane * chunks * pieces] = solved[piece]

                older = piece - LAG - tm * chunks * pieces

                @pl.when((older >= 0) & (older < chunks * pieces))
                def _():
                    hand_over(older)
        return one, two, three

    @pl.when(solver)
    def _():
        nothing = jnp.zeros((ROWS, width), F32)
        lax.fori_loop(0, planes * chunks, advance, (nothing,) * 3)

    def mate_copy(piece):
        block = out_ref.at[pl.ds(core * half, half), piece]
        return remote(block, block, mate_send.at[piece], mate_recv.at[piece], mate)

    done = jnp.where(solver, max(chunks * pieces - LAG, 0), 0)

    def finish(step, carry):
        @pl.when((step >= done) & (step < chunks * pieces))
        def _():
            hand_over(step)

        @pl.when(step > 0)
        def _():
            piece = step - 1

            @pl.when(jnp.logical_not(straight(piece)))
            def _():
                for turn in range(1, breadth):
                    over_copy(piece, turn).wait_recv()

            mate_copy(piece).start()

        return carry

    lax.fori_loop(0, chunks * pieces + 1, finish, 0)

    def settle(piece, carry):
        plane = lax.div(piece, chunks * pieces)
        for turn in range(depth):
            if turn:
                out_copy(piece, turn, plane).wait_send()
            else:
                @pl.when(plane != planes - 1)
                def _():
                    out_copy(piece, 0, plane).wait_send()
        return carry

    @pl.when(solver)
    def _():
        lax.fori_loop(0, planes * chunks * pieces, settle, 0)
        for turn in range(depth):
            for other in range(1, breadth):
                last_copy(turn, other).wait_send()

    def release(chunk):
        pair_copy(chunk).wait_send()
        for turn in range(1, breadth):
            side_copy(chunk, turn).wait_send()
        for turn in range(1, depth):
            sum_copy(chunk, turn).wait_send()

        @pl.when(jnp.logical_not(solver))
        def _():
            sum_copy(chunk, 0).wait_send()

    for chunk in range(count):
        if chunk < chunks:
            release(chunk)
        else:
            @pl.when(tm < planes - 1)
            def _():
                release(chunk)
    for piece in range(chunks * pieces):
        @pl.when(jnp.logical_not(straight(piece)))
        def _():
            for turn in range(1, breadth):
                over_copy(piece, turn).wait_send()

        mate_copy(piece).wait_send()
        mate_copy(piece).wait_recv()


def per_device(params, kernel, lag_offsets, observed, diag_inverse, coupling):
    samples, steps, cols = params.shape
    lags, _, sensors = kernel.shape
    band = coupling.shape[0]
    width = -(-sensors // LANES) * LANES
    depth, breadth = layout()
    planes = lax.axis_size("tm")
    chunks = steps // ROWS
    share = samples // (2 * depth * breadth)
    group = depth * share
    half = samples // 2
    pieces = ROWS // PIECE
    spills = len(spill_extents())
    vmem, dma = pltpu.VMEM, pltpu.SemaphoreType.DMA
    hbm = pl.BlockSpec(memory_space=pl.ANY)
    gathered = pl.pallas_call(
        whole_kernel,
        out_shape=jax.ShapeDtypeStruct((samples, steps // PIECE, PIECE, sensors), F32),
        in_specs=[hbm, hbm, pl.BlockSpec(memory_space=pltpu.SMEM), hbm, hbm, hbm],
        out_specs=pl.BlockSpec(memory_space=pltpu.VMEM),
        scratch_shapes=[
            vmem(params.shape, BF16),
            vmem((lags, sensors, cols), BF16),
            vmem(observed.shape, BF16),
            vmem(diag_inverse.shape, F32),
            vmem(coupling.shape, F32),
            vmem((REACH - 1 + (chunks + spills) * ROWS, samples, cols), BF16),
            vmem((chunks + spills, samples, ROWS, sensors), F32),
            vmem((chunks + spills, half, ROWS, sensors), F32),
            vmem((chunks + spills, half, ROWS, sensors), F32),
            vmem((chunks + spills, breadth - 1, group, ROWS, sensors), F32),
            vmem((chunks + spills, group, ROWS, sensors), F32),
            vmem((planes, chunks, depth, share, ROWS, sensors), F32),
            vmem((planes, spills, depth, share, ROWS, sensors), F32),
            vmem((share, steps, sensors), F32),
            vmem((width, width), F32),
            vmem((width, width), BF16),
            vmem((width, width), BF16),
            vmem((width, 2 * width), BF16),
            vmem(((band + 1) * width, 2 * width), BF16),
            vmem((share, ROWS, width), F32),
            vmem((planes * chunks * pieces, share, PIECE, sensors), F32),
            dma((5,)),
            dma((chunks + spills,)),
            dma((chunks + spills,)),
            dma((chunks + spills, breadth - 1)),
            dma((chunks + spills, breadth - 1)),
            dma((chunks + spills, depth)),
            dma((planes, chunks, depth)),
            dma((planes, spills, depth)),
            dma((planes * chunks * pieces, depth)),
            dma((chunks * pieces, depth)),
            dma((depth, breadth - 1)),
            dma((breadth - 1, depth)),
            dma((chunks * pieces, breadth - 1)),
            dma((chunks * pieces, breadth - 1)),
            dma((chunks * pieces,)),
            dma((chunks * pieces,)),
        ],
        compiler_params=pltpu.CompilerParams(
            collective_id=0, has_side_effects=True, vmem_limit_bytes=60 * 2**20
        ),
    )(params, jnp.swapaxes(kernel, 1, 2), lag_offsets, observed, diag_inverse, coupling)
    return gathered.reshape(samples, steps, sensors)


def solution(mesh):
    in_specs = (P(None, "tm", "param"), P(None, "param", None), P(), P(None, "tm", None), P(), P())
    out_specs = P(None, "tm", None)
    return jax.shard_map(
        per_device, mesh=mesh, in_specs=in_specs, out_specs=out_specs, check_vma=False
    )
```
